256 devices in a mesh: ty: 16 (over y_lo, x, core), tx: 8 (over z), mode: 2 (over y_hi).
Axes of the slice: x: 4, y: 4 (y_hi: 2, y_lo: 2; y = y_hi * 2 + y_lo), z: 8, core: 2. Of those that a mesh axis runs over, the one named last changes fastest.
Arguments:
- object_field: float32 [2, 2, 4096, 2048], P(None, None, 'ty', 'tx'), may hold values from -2.4 to 2.4
- probe: float32 [4, 256, 512], P('mode'), may hold values from -6 to 6
- patterns: float32 [128, 256, 256], P(('ty', 'tx')), may hold values from 0.2 to 3
- offsets: int32 [128, 2], P(('ty', 'tx')), may hold values from 0 to 128
- phase: float32 [256, 256], replicated, may hold values from -3.140625 to 3.140625
- past_steps: bfloat16 [5, 2, 2, 4096, 2048], P(None, None, None, 'ty', 'tx'), may hold values from -4 to 4
- past_changes: bfloat16 [5, 2, 2, 4096, 2048], P(None, None, None, 'ty', 'tx'), may hold values from -16 to 16, as said below
Outputs:
- new_object: float32 [2, 2, 4096, 2048], P(None, None, 'ty', 'tx')
- gradient: float32 [2, 2, 4096, 2048], P(None, None, 'ty', 'tx')
The draws below stay inside these ranges and needn't reach their ends.
Inputs may be any that keep to these rules, and one draw needn't show every extreme that they name: Every entry of past_changes has the sign of the same entry of past_steps.
All inputs are finite; a program needn't handle non-finite values.
Results may differ from the reference program's by a relative error of at most 0.02.
Values sent between devices are 32-bit elements; how exact they have to be, the bound alone decides.
No kernel may reach another device: no remote copies, remote signals or barrier semaphores. Data moves between devices by JAX's collectives and lax.ppermute only.
A program may use at most 64 MiB of HBM per device.

```python
import math
import jax
import jax.numpy as jnp
from jax import lax

PROBE = 256
MODES = 4
SLICES = 2
MEMORY = 5
TILE = 256
HALO = 64
P_DEV = 1
NY = 4096
NX = 2048
NPAT = 128
SPAN = 128
N_TX = 8


def object_base(key):
    object_key = jax.random.fold_in(key, 101)
    return 0.6 * jax.random.truncated_normal(object_key, -4.0, 4.0, (SLICES, 2, NY, NX), jnp.float32)


def history_steps(key):
    base = object_base(key)
    row_key = jax.random.fold_in(key, 202)
    col_key = jax.random.fold_in(key, 203)
    noise_key = jax.random.fold_in(key, 204)
    low_scale, high_scale = (0.3, 3.0)
    row_scale = jnp.exp(jax.random.uniform(row_key, (MEMORY, 1, 1, NY, 1), jnp.float32, math.log(low_scale), math.log(high_scale)))
    col_scale = jnp.exp(jax.random.uniform(col_key, (MEMORY, 1, 1, 1, NX), jnp.float32, math.log(low_scale), math.log(high_scale)))
    own_noise = jax.random.truncated_normal(noise_key, -4.0, 4.0, (MEMORY, SLICES, 2, NY, NX), jnp.float32)
    noise = own_noise
    return 0.3 * (base[None] + 0.3 * noise * row_scale * col_scale)


def draw_object_field(key, part):
    return object_base(key)


def draw_past_steps(key, part):
    return history_steps(key).astype(jnp.bfloat16)


def draw_past_changes(key, part):
    steps = history_steps(key).astype(jnp.bfloat16).astype(jnp.float32)
    curvature = jnp.exp(jax.random.uniform(jax.random.fold_in(key, 303), steps.shape, jnp.float32, math.log(0.5), math.log(4.0)))
    return (curvature * steps).astype(jnp.bfloat16)


def with_ends(array, rng, low, largest):
    longest = array.shape.index(max(array.shape))
    spots = []
    for shift in (0, 1):
        where = [jax.random.randint(jax.random.fold_in(rng, axis), (), 0, length) for axis, length in enumerate(array.shape)]
        where[longest] = (where[longest] + shift) % array.shape[longest]
        spots.append(tuple(where))
    return array.at[spots[0]].set(low).at[spots[1]].set(largest)


def block_levels(stream_key, extent, cuts, low, high):
    factor_of, own = 1.0, jax.random.fold_in(stream_key, 6)
    for position, parts in cuts:
        steps = jnp.exp(jax.random.uniform(jax.random.fold_in(own, position), (parts,), jnp.float32, low / len(cuts), high / len(cuts)))
        factor_of = factor_of * jnp.repeat(steps, extent[position] // parts).reshape([-1 if axis == position else 1 for axis in range(len(extent))])
    return factor_of


def gaussian(key, extent, scale, reach, split=(), held_as=jnp.bfloat16):
    values = scale * jax.random.normal(key, extent, jnp.float32)
    if split:
        values = values * block_levels(key, extent, split, -0.22, 0.18)
    return jnp.clip(values, -reach, reach).astype(held_as)


def setup_inputs(seed: int = 0) -> dict:
    splits = jax.random.split(jax.random.key(seed), 8)
    object_field = draw_object_field(jax.random.fold_in(splits[7], 71), 0)
    probe = gaussian(splits[1], (MODES, PROBE, 2 * PROBE), 1.0, 6.0, ((0, 2),), jnp.float32)
    patterns = jnp.clip(jnp.exp(math.log(3.0) - 2.7080502 * jax.random.uniform(splits[2], (NPAT, PROBE, PROBE), jnp.float32) ** block_levels(splits[2], (NPAT, PROBE, PROBE), ((0, 128),), -0.2, 0.2)), 0.2, 3.0)
    offsets = with_ends(jax.random.randint(splits[3], (NPAT, 2), 0, SPAN + 1), jax.random.fold_in(splits[3], 1), 0, SPAN).astype(jnp.int32)
    phase = jnp.clip(jax.random.uniform(splits[4], (PROBE, PROBE), jnp.float32, -3.140625, 3.140625), -3.140625, 3.140625)
    past_steps = draw_past_steps(jax.random.fold_in(splits[7], 71), 0)
    past_changes = draw_past_changes(jax.random.fold_in(splits[7], 71), 0)
    return dict(object_field=object_field, probe=probe, patterns=patterns, offsets=offsets, phase=phase, past_steps=past_steps, past_changes=past_changes)


REG_WEIGHT = 1.0

def dft_tables(length):
    indices = jnp.arange(length, dtype=jnp.int32)
    products = indices[:, None] * indices[None, :] % length
    angles = products.astype(jnp.float32) * (2.0 * math.pi / length)
    cosine_table = jnp.cos(angles) / math.sqrt(length)
    sine_table = jnp.sin(angles) / math.sqrt(length)
    forward_right = jnp.concatenate([jnp.concatenate([cosine_table, -sine_table], 1), jnp.concatenate([sine_table, cosine_table], 1)], 0)
    inverse_right = jnp.concatenate([jnp.concatenate([cosine_table, sine_table], 1), jnp.concatenate([-sine_table, cosine_table], 1)], 0)
    left_table = jnp.concatenate([cosine_table, sine_table], 0)
    return (forward_right.astype(jnp.bfloat16), inverse_right.astype(jnp.bfloat16), left_table.astype(jnp.bfloat16))

def transform(wavefield, tables, inverse):
    right_table = tables[1] if inverse else tables[0]
    sign_value = -1.0 if inverse else 1.0
    lead_shape = wavefield.shape[:-2]
    length = wavefield.shape[-2]
    flat_wave = wavefield.reshape(-1, 2 * length).astype(jnp.bfloat16)
    first_pass = jnp.dot(flat_wave, right_table, preferred_element_type=jnp.float32)
    first_pass = first_pass.reshape(-1, length, 2 * length).astype(jnp.bfloat16)
    second_pass = jnp.einsum('jk,bkl->bjl', tables[2].astype(jnp.float32), first_pass.astype(jnp.float32), precision=lax.Precision.HIGHEST)
    upper = second_pass[:, :length]
    lower = second_pass[:, length:]
    real_part = upper[:, :, :length] + sign_value * lower[:, :, length:]
    imag_part = upper[:, :, length:] - sign_value * lower[:, :, :length]
    return jnp.concatenate([real_part, imag_part], -1).reshape(lead_shape + (length, 2 * length))

def complex_product(first, second, conjugate_first):
    length = first.shape[-1] // 2
    first_real = first[..., :length]
    first_imag = first[..., length:]
    if conjugate_first:
        first_imag = -first_imag
    second_real = second[..., :length]
    second_imag = second[..., length:]
    return jnp.concatenate([first_real * second_real - first_imag * second_imag, first_real * second_imag + first_imag * second_real], -1)

def propagate(wavefield, kernel, tables, adjoint):
    spectrum = transform(wavefield, tables, False)
    spectrum = complex_product(kernel, spectrum, adjoint)
    return transform(spectrum, tables, True)

def forward_waves(windows, probe, kernel, tables):
    slice_count = windows.shape[1]
    wavefield = jnp.broadcast_to(probe[None], (windows.shape[0],) + probe.shape)
    entering = []
    for slice_index in range(slice_count):
        entering.append(wavefield)
        wavefield = complex_product(windows[:, slice_index][:, None], wavefield, False)
        if slice_index + 1 < slice_count:
            wavefield = propagate(wavefield, kernel, tables, False)
    return (transform(wavefield, tables, False), entering)

def window_gradients(far_field, entering, windows, residual, kernel, tables):
    slice_count = windows.shape[1]
    doubled = jnp.concatenate([residual, residual], -1)[:, None]
    adjoint_wave = transform(2.0 / MODES * doubled * far_field, tables, True)
    pieces = []
    for slice_index in reversed(range(slice_count)):
        pieces.append(lax.optimization_barrier(jnp.sum(complex_product(entering[slice_index], adjoint_wave, True), axis=1)))
        if slice_index > 0:
            adjoint_wave = complex_product(windows[:, slice_index][:, None], adjoint_wave, True)
            adjoint_wave = propagate(adjoint_wave, kernel, tables, True)
    return jnp.stack(pieces[::-1], 1)

def inner_product(first, second):
    return jnp.sum(first.astype(jnp.float32) * second.astype(jnp.float32))

def reference(object_field, probe, patterns, offsets, phase, past_steps, past_changes):
    probe_edge = probe.shape[1]
    rows_total = object_field.shape[2]
    cols_total = object_field.shape[3]
    tables = dft_tables(probe_edge)
    kernel = jnp.concatenate([jnp.cos(phase), jnp.sin(phase)], -1)
    span_ids = jnp.arange(probe_edge, dtype=jnp.int32)

    def one_pattern(collected, inputs):
        pattern, offset, pattern_index = inputs
        device = pattern_index // P_DEV
        row_start = TILE * (device // N_TX) - HALO + offset[0]
        col_start = TILE * (device % N_TX) - HALO + offset[1]
        row_ids = ((row_start + span_ids) % rows_total).astype(jnp.int32)
        col_ids = ((col_start + span_ids) % cols_total).astype(jnp.int32)
        window = object_field[:, :, row_ids[:, None], col_ids[None, :]]
        packed = jnp.concatenate([window[:, 0], window[:, 1]], -1)[None]
        far_field, entering = forward_waves(packed, probe, kernel, tables)
        intensity = lax.optimization_barrier(jnp.sum(far_field[..., :probe_edge] ** 2 + far_field[..., probe_edge:] ** 2, axis=1)) / MODES
        residual = intensity - pattern[None]
        pieces = window_gradients(far_field, entering, packed, residual, kernel, tables)[0]
        unpacked = jnp.stack([pieces[..., :probe_edge], pieces[..., probe_edge:]], 1)
        collected = collected.at[:, :, row_ids[:, None], col_ids[None, :]].add(unpacked)
        return (collected, None)
    zero_field = jnp.zeros(object_field.shape, jnp.float32)
    pattern_ids = jnp.arange(patterns.shape[0], dtype=jnp.int32)
    collected, unused = lax.scan(one_pattern, zero_field, (patterns, offsets, pattern_ids))
    gradient = collected + REG_WEIGHT * object_field
    memory = past_steps.shape[0]
    curvatures = [inner_product(past_steps[history_index], past_changes[history_index]) for history_index in range(memory)]
    search = gradient
    alphas = [None] * memory
    for history_index in reversed(range(memory)):
        alphas[history_index] = inner_product(past_steps[history_index], search) / curvatures[history_index]
        search = search - alphas[history_index] * past_changes[history_index].astype(jnp.float32)
    scaling = curvatures[memory - 1] / inner_product(past_changes[memory - 1], past_changes[memory - 1])
    search = scaling * search
    for history_index in range(memory):
        beta_value = inner_product(past_changes[history_index], search) / curvatures[history_index]
        search = search + (alphas[history_index] - beta_value) * past_steps[history_index].astype(jnp.float32)
    new_object = object_field - search
    return (new_object, gradient)
```

```python
import math

import jax
import jax.numpy as jnp
import numpy as np
from jax import lax
from jax.experimental import pallas as pl
from jax.experimental.pallas import tpu as pltpu
from jax.sharding import PartitionSpec as P

MODES = 4
HALO = 64
REG_WEIGHT = 1.0
N = 256
FRAME = N + 2 * HALO
MEM = 5
CHUNK = 32
F32 = jnp.float32
BF16 = jnp.bfloat16
TILES = ("ty", "tx")
VMEM = pl.BlockSpec(memory_space=pltpu.VMEM)
SMEM = pl.BlockSpec(memory_space=pltpu.SMEM)
PARAMS = pltpu.CompilerParams(vmem_limit_bytes=40 * 1024 * 1024)
SY_PAIRS = [(i, j) for i in range(MEM) for j in range(i, MEM)]
SY_ROW = {pair: k for k, pair in enumerate(SY_PAIRS)}
YY_ROW = {pair: len(SY_PAIRS) + k for k, pair in enumerate(SY_PAIRS)}
SG_ROW = 2 * len(SY_PAIRS)
YG_ROW = SG_ROW + MEM
ROWS = YG_ROW + MEM


def dft_tables():
    indices = np.arange(N, dtype=np.int32)
    products = indices[:, None] * indices[None, :] % N
    angles = products.astype(np.float32) * np.float32(2.0 * math.pi / N)
    cosine = (np.cos(angles) / np.float32(math.sqrt(N))).astype(np.float32)
    sine = (np.sin(angles) / np.float32(math.sqrt(N))).astype(np.float32)
    forward = np.block([[cosine, -sine], [sine, cosine]])
    inverse = np.block([[cosine, sine], [-sine, cosine]])
    left = np.concatenate([cosine, sine], 1)
    return tuple(jnp.asarray(t, BF16) for t in (forward, inverse, left))


def lanes(shape):
    return lax.broadcasted_iota(jnp.int32, shape, len(shape) - 1)


def chunks(total=N, step=CHUNK):
    return [slice(c, c + step) for c in range(0, total, step)]


def aligned(offset):
    base = pl.multiple_of((offset // 8) * 8, 8)
    return base, offset - base


def product(a, b, conjugate):
    ar, ai = a
    br, bi = b
    if conjugate:
        return ar * br + ai * bi, ar * bi - ai * br
    return ar * br - ai * bi, ar * bi + ai * br


def halves(ref, index, rows):
    return ref[index, rows, 0:N], ref[index, rows, N : 2 * N]


def first_pass(xb, ks, m, right, inverse):
    y = jnp.dot(xb[m], right[...], preferred_element_type=F32).astype(BF16)
    yr, yi = y[:, :N], y[:, N:]
    ks[m, 0:N, :] = y
    if inverse:
        ks[m, N : 2 * N, 0:N] = -yi
        ks[m, N : 2 * N, N : 2 * N] = yr
    else:
        ks[m, N : 2 * N, 0:N] = yi
        ks[m, N : 2 * N, N : 2 * N] = -yr


def second_pass(ks, m, left):
    return jnp.dot(left[...], ks[m], preferred_element_type=F32)


def propagate(xb, ks, zs, m, kernel, tables, adjoint):
    forward, inverse, left = tables
    first_pass(xb, ks, m, forward, False)
    zs[m] = second_pass(ks, m, left)
    for rows in chunks():
        h = (kernel[0, rows, :], kernel[1, rows, :])
        re, im = product(h, halves(zs, m, rows), adjoint)
        xb[m, rows, 0:N] = re.astype(BF16)
        xb[m, rows, N : 2 * N] = im.astype(BF16)
    first_pass(xb, ks, m, inverse, True)
    return second_pass(ks, m, left)


def forward_mode(m, psi0, window, kernel, tables, psi1, far, xb, ks, zs):
    forward, inverse, left = tables
    for rows in chunks():
        re, im = product(halves(window, 0, rows), (psi0[rows, 0:N], psi0[rows, N : 2 * N]), False)
        xb[m, rows, 0:N] = re.astype(BF16)
        xb[m, rows, N : 2 * N] = im.astype(BF16)
    psi1[m] = propagate(xb, ks, zs, m, kernel, tables, False)
    for rows in chunks():
        re, im = product(halves(window, 1, rows), halves(psi1, m, rows), False)
        xb[m, rows, 0:N] = re.astype(BF16)
        xb[m, rows, N : 2 * N] = im.astype(BF16)
    first_pass(xb, ks, m, forward, False)
    far[m] = second_pass(ks, m, left)


def add_intensity(far, out, base):
    for rows in chunks():
        terms = []
        for m in range(2):
            re, im = halves(far, m, rows)
            terms.append(re * re + im * im)
        total = terms[0] + terms[1]
        out[rows, :] = total if base is None else base[rows, :] + total


def own_kernel(offsets, obj, top, bottom, left_in, right_in, corner_left, corner_right, probe, kernel,
               fwd_t, inv_t, left_t, window, psi1, far, intensity, ext, xb, ks, zs):
    tables = (fwd_t, inv_t, left_t)
    low = lanes((HALO, 2 * HALO)) < HALO

    def border(right_block, left_block, part):
        if part == 0:
            return jnp.where(low, right_block, pltpu.roll(left_block, HALO, 1))
        return jnp.where(low, pltpu.roll(right_block, HALO, 1), left_block)

    row_base, row_rest = aligned(offsets[0, 0])
    shift = lax.rem(HALO + FRAME - offsets[0, 1], FRAME)
    for s in range(2):
        for part in range(2):
            q = 2 * s + part
            ext[q, 0:HALO, 0:N] = top[s, part]
            ext[q, HALO : HALO + N, 0:N] = obj[s, part]
            ext[q, HALO + N : FRAME, 0:N] = bottom[s, part]
            ext[q, 0:HALO, N:FRAME] = border(
                corner_right[s, HALO : 2 * HALO], corner_left[s, HALO : 2 * HALO], part)
            ext[q, HALO + N : FRAME, N:FRAME] = border(
                corner_right[s, 0:HALO], corner_left[s, 0:HALO], part)
            for rows in chunks(N, HALO):
                ext[q, HALO + rows.start : HALO + rows.stop, N:FRAME] = border(
                    right_in[s, rows], left_in[s, rows], part)
            for rows in chunks(N, 64):
                block = ext[q, pl.ds(row_base + rows.start, 72), :]
                block = pltpu.roll(block, lax.rem(72 - row_rest, 72), 0)[:64]
                window[s, rows, part * N : (part + 1) * N] = pltpu.roll(block, shift, 1)[:, :N]
    for m in range(2):
        forward_mode(m, probe.at[m], window, kernel, tables, psi1, far, xb, ks, zs)
    add_intensity(far, intensity, None)


def other_kernel(offsets, obj, probe, near, swapped, kernel, fwd_t, inv_t, left_t, patterns, window,
                 psi1_own, far_own, intensity, gradient, row_top, row_bottom, col_left, col_right,
                 corner_left, corner_right, psi1, far, inten, xb, ks, zs, back, frame):
    tables = (fwd_t, inv_t, left_t)
    others = (near, swapped)
    for m in range(2):
        forward_mode(m, others[m], window, kernel, tables, psi1, far, xb, ks, zs)
    add_intensity(far, inten, intensity)
    for rows in chunks():
        inten[rows, :] = (inten[rows, :] * (1.0 / MODES) - patterns[0, rows, :]) * (2.0 / MODES)
    row_base, row_rest = aligned(offsets[0, 0])
    shift = lax.rem(HALO + N + offsets[0, 1], FRAME)
    for pair in range(2):
        far_now = far_own if pair == 0 else far
        psi_now = psi1_own if pair == 0 else psi1
        first = (probe.at[0], probe.at[1]) if pair == 0 else others
        for m in range(2):
            for rows in chunks():
                scale = inten[rows, :]
                re, im = halves(far_now, m, rows)
                xb[m, rows, 0:N] = (scale * re).astype(BF16)
                xb[m, rows, N : 2 * N] = (scale * im).astype(BF16)
            first_pass(xb, ks, m, inv_t, True)
            zs[m] = second_pass(ks, m, left_t)
            for rows in chunks():
                current = halves(zs, m, rows)
                re, im = product(halves(psi_now, m, rows), current, True)
                if pair or m:
                    re, im = re + back[1, rows, 0:N], im + back[1, rows, N : 2 * N]
                back[1, rows, 0:N] = re
                back[1, rows, N : 2 * N] = im
                re, im = product(halves(window, 1, rows), current, True)
                xb[m, rows, 0:N] = re.astype(BF16)
                xb[m, rows, N : 2 * N] = im.astype(BF16)
            zs[m] = propagate(xb, ks, zs, m, kernel, tables, True)
            for rows in chunks():
                psi0 = first[m]
                re, im = product((psi0[rows, 0:N], psi0[rows, N : 2 * N]), halves(zs, m, rows), True)
                if pair or m:
                    re, im = re + back[0, rows, 0:N], im + back[0, rows, N : 2 * N]
                back[0, rows, 0:N] = re
                back[0, rows, N : 2 * N] = im
    low = lanes((HALO, 2 * HALO)) < HALO
    zero = jnp.zeros((HALO, 2 * HALO), F32)
    gap = jnp.zeros((8, FRAME), F32)
    frame[...] = jnp.zeros(frame.shape, F32)
    for q in range(4):
        s, part = divmod(q, 2)
        for rows in chunks(N, 64):
            block = back[s, rows, part * N : (part + 1) * N]
            block = pltpu.roll(jnp.concatenate([block, zero], 1), shift, 1)
            block = pltpu.roll(jnp.concatenate([block, gap], 0), row_rest, 0)
            frame[q, pl.ds(row_base + rows.start, 72), :] += block
    for s in range(2):
        for part in range(2):
            q = 2 * s + part
            gradient[s, part] = frame[q, HALO : HALO + N, 0:N] + REG_WEIGHT * obj[s, part]
            row_top[s, part] = frame[q, 0:HALO, 0:N]
            row_bottom[s, part] = frame[q, HALO + N : FRAME, 0:N]

        def strips(rows):
            re, im = frame[2 * s, rows, N:FRAME], frame[2 * s + 1, rows, N:FRAME]
            right = jnp.where(low, re, pltpu.roll(im, HALO, 1))
            left = jnp.where(low, pltpu.roll(re, HALO, 1), im)
            return right, left

        for rows in chunks(N, HALO):
            right, left = strips(slice(HALO + rows.start, HALO + rows.stop))
            col_right[s, rows] = right
            col_left[s, rows] = left
        right, left = strips(slice(HALO + N, FRAME))
        corner_right[s, 0:HALO] = right
        corner_left[s, 0:HALO] = left
        right, left = strips(slice(0, HALO))
        corner_right[s, HALO : 2 * HALO] = right
        corner_left[s, HALO : 2 * HALO] = left


def put_rows(out, first_row, sums):
    for k, value in enumerate(sums):
        out[first_row + k : first_row + k + 1, :] = jnp.sum(value, axis=0, keepdims=True)


def fold(value):
    rows = value.shape[0]
    value = value[:, : N // 2] + value[:, N // 2 :]
    return sum(value[r : r + 8] for r in range(0, rows, 8))


def gram_kernel(steps, changes, out):
    count = 2 * len(SY_PAIRS)

    def body(k, carry):
        q = k // (N // 16)
        rows = pl.ds((k % (N // 16)) * 16, 16)
        s, part = q // 2, q % 2
        st = [steps[i, s, part, rows, :].astype(F32) for i in range(MEM)]
        ch = [changes[i, s, part, rows, :].astype(F32) for i in range(MEM)]
        new = [fold(st[i] * ch[j]) for i, j in SY_PAIRS] + [fold(ch[i] * ch[j]) for i, j in SY_PAIRS]
        return tuple(a + b for a, b in zip(carry, new))

    zero = tuple(jnp.zeros((8, N // 2), F32) for _ in range(count))
    put_rows(out, 0, lax.fori_loop(0, 4 * (N // 16), body, zero))


def dots_kernel(gradient_in, row_up, row_down, col_left, col_right, steps, changes, gram, gradient, out, sums):
    low = lanes((N, 2 * HALO)) < HALO
    for s in range(2):
        for part in range(2):
            gradient[s, part] = gradient_in[s, part]
            gradient[s, part, 0:HALO, :] += row_up[s, part]
            gradient[s, part, N - HALO : N, :] += row_down[s, part]
        from_left, from_right = col_left[s], col_right[s]
        flip_left, flip_right = pltpu.roll(from_left, HALO, 1), pltpu.roll(from_right, HALO, 1)
        for part in range(2):
            a = from_left if part == 0 else flip_left
            b = flip_right if part == 0 else from_right
            gradient[s, part, :, 0 : 2 * HALO] += jnp.where(low, a, 0.0)
            gradient[s, part, :, N - 2 * HALO : N] += jnp.where(low, 0.0, b)

    def body(k, carry):
        q = k // (N // 16)
        rows = pl.ds((k % (N // 16)) * 16, 16)
        s, part = q // 2, q % 2
        g = gradient[s, part, rows, :]
        new = [fold(steps[i, s, part, rows, :].astype(F32) * g) for i in range(MEM)]
        new += [fold(changes[i, s, part, rows, :].astype(F32) * g) for i in range(MEM)]
        return tuple(a + b for a, b in zip(carry, new))

    zero = tuple(jnp.zeros((8, N // 2), F32) for _ in range(2 * MEM))
    sums[...] = jnp.zeros(sums.shape, F32)
    sums[0:SG_ROW, :] = gram[0:SG_ROW, :]
    put_rows(sums, SG_ROW, lax.fori_loop(0, 4 * (N // 16), body, zero))
    totals = jnp.sum(sums[...], axis=1, keepdims=True)
    row = lax.broadcasted_iota(jnp.int32, (128, 128), 0)
    spread = jnp.where(row == lanes((128, 128)), totals, 0.0)
    total_row = jnp.sum(spread, axis=0, keepdims=True)
    out[...] = jnp.broadcast_to(total_row[None], (128, 1, 128))


def final_kernel(parts, obj, gradient, steps, changes, out):
    total = jnp.sum(parts[:, 0, :], axis=0, keepdims=True)
    row = lax.broadcasted_iota(jnp.int32, (128, 128), 0)
    diagonal = jnp.where(row == lanes((128, 128)), total, 0.0)
    splats = jnp.broadcast_to(jnp.sum(diagonal, axis=1, keepdims=True), (128, 128))

    def value(k):
        return splats[k : k + 1, :]

    sy = {pair: value(k) for pair, k in SY_ROW.items()}
    yy = {pair: value(k) for pair, k in YY_ROW.items()}
    inverse = [1.0 / sy[i, i] for i in range(MEM)]
    scaling = sy[MEM - 1, MEM - 1] / yy[MEM - 1, MEM - 1]
    alpha = [None] * MEM
    for i in reversed(range(MEM)):
        term = value(SG_ROW + i)
        for j in reversed(range(i + 1, MEM)):
            term = term - alpha[j] * sy[i, j]
        alpha[i] = term * inverse[i]
    weights = []
    for i in range(MEM):
        term = value(YG_ROW + i)
        for j in reversed(range(MEM)):
            term = term - alpha[j] * yy[min(i, j), max(i, j)]
        term = scaling * term
        for j in range(i):
            term = term + weights[j] * sy[j, i]
        weights.append(alpha[i] - term * inverse[i])

    def wide(x):
        return jnp.broadcast_to(jnp.concatenate([x, x], 1), (16, N))

    scale = wide(scaling)
    step_weights = [wide(w) for w in weights]
    change_weights = [wide(scaling * a) for a in alpha]

    def body(k, carry):
        q = k // (N // 16)
        rows = pl.ds((k % (N // 16)) * 16, 16)
        s, part = q // 2, q % 2
        acc = scale * gradient[s, part, rows, :]
        for j in range(MEM):
            acc = acc - change_weights[j] * changes[j, s, part, rows, :].astype(F32)
            acc = acc + step_weights[j] * steps[j, s, part, rows, :].astype(F32)
        out[s, part, rows, :] = obj[s, part, rows, :] - acc
        return carry

    lax.fori_loop(0, 4 * (N // 16), body, 0)


def shape(*dims, dtype=F32):
    return jax.ShapeDtypeStruct(dims, dtype)


def scratch(*dims, dtype=F32):
    return pltpu.VMEM(dims, dtype)


def call(kernel, outs, scratches, args, smem=0):
    return pl.pallas_call(
        kernel,
        out_shape=outs,
        in_specs=[SMEM] * smem + [VMEM] * (len(args) - smem),
        out_specs=jax.tree.map(lambda _: VMEM, outs),
        scratch_shapes=scratches,
        compiler_params=PARAMS,
    )(*args)


def shifted(value, axis, step):
    size = lax.axis_size(axis)
    return lax.ppermute(value, axis, [(i, (i + step) % size) for i in range(size)])


def packed(value, columns):
    return jnp.concatenate([value[:, 0, :, columns], value[:, 1, :, columns]], -1)


def near_pairs(rows, modes):
    half = rows // modes
    pairs = []
    for t in range(rows):
        for m in range(modes):
            y = m * modes + t // half
            other = 2 * modes - 1 - y
            target = (other % modes) * half + t % half
            pairs.append((t * modes + m, target * modes + other // modes))
    return pairs


def per_device(object_field, probe, patterns, offsets, phase, past_steps, past_changes):
    rows_axis, modes_axis = lax.axis_size("ty"), lax.axis_size("mode")
    core = lax.axis_index("ty") % 2
    tables = dft_tables()
    kernel = jnp.stack([jnp.cos(phase), jnp.sin(phase)])
    chosen = lax.dynamic_slice_in_dim(probe, core, 1, 0)[0]
    near = lax.ppermute(chosen, ("ty", "mode"), near_pairs(rows_axis, modes_axis))
    first, last = slice(0, HALO), slice(N - HALO, N)
    top = shifted(object_field[:, :, last, :], "ty", 1)
    bottom = shifted(object_field[:, :, first, :], "ty", -1)
    left = shifted(packed(object_field, last), "tx", 1)
    right = shifted(packed(object_field, first), "tx", -1)
    strips = jnp.concatenate([bottom, top], 2)
    corner_left = shifted(packed(strips, last), "tx", 1)
    corner_right = shifted(packed(strips, first), "tx", -1)
    near, left, right, corner_left, corner_right = lax.optimization_barrier(
        (near, left, right, corner_left, corner_right))
    swapped = lax.ppermute(near, "ty", [(i, i ^ 1) for i in range(rows_axis)])
    gram = call(gram_kernel, shape(32, 128), [], (past_steps, past_changes))
    work = [scratch(2, N, 2 * N, dtype=BF16), scratch(2, 2 * N, 2 * N, dtype=BF16), scratch(2, N, 2 * N)]
    window, psi1, far, intensity = call(
        own_kernel,
        (shape(2, N, 2 * N), shape(2, N, 2 * N), shape(2, N, 2 * N), shape(N, N)),
        [scratch(4, FRAME + 8, FRAME)] + work,
        (offsets, object_field, top, bottom, left, right, corner_left, corner_right, probe, kernel) + tables,
        smem=1,
    )
    strip, side, corner = shape(2, 2, HALO, N), shape(2, N, 2 * HALO), shape(2, 2 * HALO, 2 * HALO)
    partial, row_top, row_bottom, col_left, col_right, corner_left, corner_right = call(
        other_kernel,
        (shape(2, 2, N, N), strip, strip, side, side, corner, corner),
        [scratch(2, N, 2 * N), scratch(2, N, 2 * N), scratch(N, N)] + work
        + [scratch(2, N, 2 * N), scratch(4, FRAME + 8, FRAME)],
        (offsets, object_field, probe, near, swapped, kernel) + tables
        + (patterns, window, psi1, far, intensity),
        smem=1,
    )
    from_left = shifted(corner_right, "tx", 1)
    from_right = shifted(corner_left, "tx", -1)
    side_left = shifted(col_right, "tx", 1)
    side_right = shifted(col_left, "tx", -1)

    def with_corners(strip_now, rows):
        def unpacked(block):
            return jnp.stack([block[:, rows, :HALO], block[:, rows, HALO:]], 1)

        gap = jnp.zeros(strip_now.shape[:3] + (N - 2 * HALO,), F32)
        return strip_now + jnp.concatenate([unpacked(from_left), gap, unpacked(from_right)], -1)

    row_up = shifted(with_corners(row_bottom, slice(0, HALO)), "ty", 1)
    row_down = shifted(with_corners(row_top, slice(HALO, 2 * HALO)), "ty", -1)
    gradient, sums = call(
        dots_kernel,
        (shape(2, 2, N, N), shape(128, 1, 128)),
        [scratch(128, 128)],
        (partial, row_up, row_down, side_left, side_right, past_steps, past_changes, gram),
    )
    parts = lax.all_to_all(sums, TILES, 0, 0)
    new_object = call(
        final_kernel, shape(2, 2, N, N), [], (parts, object_field, gradient, past_steps, past_changes))
    return (new_object, gradient)


def solution(mesh):
    placed = (
        P(None, None, "ty", "tx"),
        P("mode", None, None),
        P(TILES, None, None),
        P(TILES, None),
        P(),
        P(None, None, None, "ty", "tx"),
        P(None, None, None, "ty", "tx"),
    )
    return jax.shard_map(
        per_device,
        mesh=mesh,
        in_specs=placed,
        out_specs=(P(None, None, "ty", "tx"), P(None, None, "ty", "tx")),
        check_vma=False,
    )
```

```python
import math

import jax
import jax.numpy as jnp
import numpy as np
from jax import lax
from jax.experimental import pallas as pl
from jax.experimental.pallas import tpu as pltpu
from jax.sharding import PartitionSpec as P

MODES = 4
HALO = 64
REG_WEIGHT = 1.0
N = 256
FRAME = N + 2 * HALO
MEM = 5
CHUNK = 32
F32 = jnp.float32
BF16 = jnp.bfloat16
TILES = ("ty", "tx")
VMEM = pl.BlockSpec(memory_space=pltpu.VMEM)
ANY = pl.BlockSpec(memory_space=pltpu.HBM)
SMEM = pl.BlockSpec(memory_space=pltpu.SMEM)
PARAMS = pltpu.CompilerParams(vmem_limit_bytes=40 * 1024 * 1024)
SY_PAIRS = [(i, j) for i in range(MEM) for j in range(i, MEM)]
SY_ROW = {pair: k for k, pair in enumerate(SY_PAIRS)}
YY_ROW = {pair: len(SY_PAIRS) + k for k, pair in enumerate(SY_PAIRS)}
SG_ROW = 2 * len(SY_PAIRS)
YG_ROW = SG_ROW + MEM
ROWS = YG_ROW + MEM


def dft_tables():
    indices = np.arange(N, dtype=np.int32)
    products = indices[:, None] * indices[None, :] % N
    angles = products.astype(np.float32) * np.float32(2.0 * math.pi / N)
    cosine = (np.cos(angles) / np.float32(math.sqrt(N))).astype(np.float32)
    sine = (np.sin(angles) / np.float32(math.sqrt(N))).astype(np.float32)
    forward = np.block([[cosine, -sine], [sine, cosine]])
    inverse = np.block([[cosine, sine], [-sine, cosine]])
    left = np.concatenate([cosine, sine], 1)
    return tuple(jnp.asarray(t, BF16) for t in (forward, inverse, left))


def lanes(shape):
    return lax.broadcasted_iota(jnp.int32, shape, len(shape) - 1)


def chunks(total=N, step=CHUNK):
    return [slice(c, c + step) for c in range(0, total, step)]


def aligned(offset):
    base = pl.multiple_of((offset // 8) * 8, 8)
    return base, offset - base


def product(a, b, conjugate):
    ar, ai = a
    br, bi = b
    if conjugate:
        return ar * br + ai * bi, ar * bi - ai * br
    return ar * br - ai * bi, ar * bi + ai * br


def halves(ref, index, rows):
    return ref[index, rows, 0:N], ref[index, rows, N : 2 * N]


def first_pass(xb, ks, m, right, inverse):
    y = jnp.dot(xb[m], right[...], preferred_element_type=F32).astype(BF16)
    yr, yi = y[:, :N], y[:, N:]
    ks[m, 0:N, :] = y
    if inverse:
        ks[m, N : 2 * N, 0:N] = -yi
        ks[m, N : 2 * N, N : 2 * N] = yr
    else:
        ks[m, N : 2 * N, 0:N] = yi
        ks[m, N : 2 * N, N : 2 * N] = -yr


def second_pass(ks, m, left):
    return jnp.dot(left[...], ks[m], preferred_element_type=F32)


def propagate(xb, ks, zs, m, kernel, tables, adjoint):
    forward, inverse, left = tables
    first_pass(xb, ks, m, forward, False)
    yield
    zs[m] = second_pass(ks, m, left)
    yield
    for rows in chunks():
        h = (kernel[0, rows, :], kernel[1, rows, :])
        re, im = product(h, halves(zs, m, rows), adjoint)
        xb[m, rows, 0:N] = re.astype(BF16)
        xb[m, rows, N : 2 * N] = im.astype(BF16)
    yield
    first_pass(xb, ks, m, inverse, True)
    yield


def forward_mode(m, psi0, window, kernel, tables, psi1, far, xb, ks, zs):
    forward, inverse, left = tables
    for rows in chunks():
        re, im = product(halves(window, 0, rows), (psi0[rows, 0:N], psi0[rows, N : 2 * N]), False)
        xb[m, rows, 0:N] = re.astype(BF16)
        xb[m, rows, N : 2 * N] = im.astype(BF16)
    yield
    yield from propagate(xb, ks, zs, m, kernel, tables, False)
    psi1[m] = second_pass(ks, m, left)
    yield
    for rows in chunks():
        re, im = product(halves(window, 1, rows), halves(psi1, m, rows), False)
        xb[m, rows, 0:N] = re.astype(BF16)
        xb[m, rows, N : 2 * N] = im.astype(BF16)
    yield
    first_pass(xb, ks, m, forward, False)
    yield
    far[m] = second_pass(ks, m, left)
    yield


def backward_mode(slot, psi0, psi1, far, scale, window, kernel, tables, pieces, xb, ks, zs):
    forward, inverse, left = tables
    pair, m = divmod(slot, 2)
    k = slot

    def collect(s, rows, re, im):
        if m:
            re, im = re + pieces[pair, s, rows, 0:N], im + pieces[pair, s, rows, N : 2 * N]
        pieces[pair, s, rows, 0:N] = re
        pieces[pair, s, rows, N : 2 * N] = im

    for rows in chunks():
        factor = scale[rows, :]
        re, im = (far[rows, 0:N], far[rows, N : 2 * N])
        xb[k, rows, 0:N] = (factor * re).astype(BF16)
        xb[k, rows, N : 2 * N] = (factor * im).astype(BF16)
    yield
    first_pass(xb, ks, k, inverse, True)
    yield
    zs[k] = second_pass(ks, k, left)
    yield
    for rows in chunks():
        current = halves(zs, k, rows)
        collect(1, rows, *product((psi1[rows, 0:N], psi1[rows, N : 2 * N]), current, True))
        re, im = product(halves(window, 1, rows), current, True)
        xb[k, rows, 0:N] = re.astype(BF16)
        xb[k, rows, N : 2 * N] = im.astype(BF16)
    yield
    yield from propagate(xb, ks, zs, k, kernel, tables, True)
    zs[k] = second_pass(ks, k, left)
    yield
    for rows in chunks():
        collect(0, rows, *product((psi0[rows, 0:N], psi0[rows, N : 2 * N]), halves(zs, k, rows), True))
    yield


def interleave(tasks):
    waiting, running = list(tasks), []
    while waiting or running:
        if waiting:
            running.append(waiting.pop(0))
        running = [task for task in running if next(task, running) is not running]


def add_intensity(far, out):
    for rows in chunks():
        terms = []
        for m in range(2):
            re, im = halves(far, m, rows)
            terms.append(re * re + im * im)
        out[rows, :] = terms[0] + terms[1]


def pack_kernel(core, obj, probe, row_first, row_last, col_first, col_last, chosen, edge_first, edge_last, sems):
    low = lanes((N, 2 * HALO)) < HALO
    moves = [
        (obj.at[:, :, :, 0 : 2 * HALO], edge_first),
        (obj.at[:, :, :, N - 2 * HALO : N], edge_last),
        (obj.at[:, :, 0:HALO, :], row_first),
        (obj.at[:, :, N - HALO : N, :], row_last),
        (probe.at[core[0]], chosen),
    ]
    copies = [pltpu.make_async_copy(src, dst, sems.at[k]) for k, (src, dst) in enumerate(moves)]
    for copy in copies:
        copy.start()
    copies[0].wait()
    for s in range(2):
        col_first[s] = jnp.where(low, edge_first[s, 0], pltpu.roll(edge_first[s, 1], HALO, 1))
    copies[1].wait()
    for s in range(2):
        col_last[s] = jnp.where(low, pltpu.roll(edge_last[s, 0], HALO, 1), edge_last[s, 1])
    for copy in copies[2:]:
        copy.wait()


def own_kernel(offsets, obj, top, bottom, left_in, right_in, corner_left, corner_right, probe, kernel,
               gram, fwd_t, inv_t, left_t, window, psi1, far, intensity, ext, xb, ks, zs):
    tables = (fwd_t, inv_t, left_t)
    low = lanes((HALO, 2 * HALO)) < HALO

    def border(right_block, left_block, part):
        if part == 0:
            return jnp.where(low, right_block, pltpu.roll(left_block, HALO, 1))
        return jnp.where(low, pltpu.roll(right_block, HALO, 1), left_block)

    row_base, row_rest = aligned(offsets[0, 0])
    shift = lax.rem(HALO + FRAME - offsets[0, 1], FRAME)
    for s in range(2):
        for part in range(2):
            q = 2 * s + part
            ext[q, 0:HALO, 0:N] = top[s, part]
            ext[q, HALO : HALO + N, 0:N] = obj[s, part]
            ext[q, HALO + N : FRAME, 0:N] = bottom[s, part]
            ext[q, 0:HALO, N:FRAME] = border(
                corner_right[s, HALO : 2 * HALO], corner_left[s, HALO : 2 * HALO], part)
            ext[q, HALO + N : FRAME, N:FRAME] = border(
                corner_right[s, 0:HALO], corner_left[s, 0:HALO], part)
            for rows in chunks(N, HALO):
                ext[q, HALO + rows.start : HALO + rows.stop, N:FRAME] = border(
                    right_in[s, rows], left_in[s, rows], part)
            for rows in chunks(N, 64):
                block = ext[q, pl.ds(row_base + rows.start, 72), :]
                block = pltpu.roll(block, lax.rem(72 - row_rest, 72), 0)[:64]
                window[s, rows, part * N : (part + 1) * N] = pltpu.roll(block, shift, 1)[:, :N]
    interleave(forward_mode(m, probe.at[m], window, kernel, tables, psi1, far, xb, ks, zs) for m in range(2))
    add_intensity(far, intensity)


def near_kernel(probe, kernel, fwd_t, inv_t, left_t, window, psi1, far, intensity, xb, ks, zs):
    interleave([forward_mode(0, probe, window, kernel, (fwd_t, inv_t, left_t), psi1, far, xb, ks, zs)])
    for rows in chunks():
        re, im = halves(far, 0, rows)
        intensity[rows, :] = re * re + im * im


def other_kernel(offsets, obj, probe, near, swapped, kernel, fwd_t, inv_t, left_t, patterns, window,
                 psi1_own, far_own, intensity, psi1_near, far_near, intensity_near, gradient, row_top, row_bottom,
                 col_left, col_right, corner_left, corner_right, psi1, far, inten, xb, ks, zs, back, frame):
    tables = (fwd_t, inv_t, left_t)
    interleave([forward_mode(0, swapped, window, kernel, tables, psi1, far, xb, ks, zs)])
    for rows in chunks():
        re, im = halves(far, 0, rows)
        inten[rows, :] = intensity[rows, :] + (intensity_near[rows, :] + (re * re + im * im))
    for rows in chunks():
        inten[rows, :] = (inten[rows, :] * (1.0 / MODES) - patterns[0, rows, :]) * (2.0 / MODES)
    row_base, row_rest = aligned(offsets[0, 0])
    shift = lax.rem(HALO + N + offsets[0, 1], FRAME)
    modes = [
        (probe.at[0], psi1_own.at[0], far_own.at[0]),
        (probe.at[1], psi1_own.at[1], far_own.at[1]),
        (near, psi1_near.at[0], far_near.at[0]),
        (swapped, psi1.at[0], far.at[0]),
    ]
    interleave(
        backward_mode(k, psi0, psi, wave, inten, window, kernel, tables, back, xb, ks, zs)
        for k, (psi0, psi, wave) in enumerate(modes))
    low = lanes((HALO, 2 * HALO)) < HALO
    zero = jnp.zeros((HALO, 2 * HALO), F32)
    gap = jnp.zeros((8, FRAME), F32)
    frame[...] = jnp.zeros(frame.shape, F32)
    for q in range(4):
        s, part = divmod(q, 2)
        for rows in chunks(N, 64):
            columns = slice(part * N, (part + 1) * N)
            block = back[0, s, rows, columns] + back[1, s, rows, columns]
            block = pltpu.roll(jnp.concatenate([block, zero], 1), shift, 1)
            block = pltpu.roll(jnp.concatenate([block, gap], 0), row_rest, 0)
            frame[q, pl.ds(row_base + rows.start, 72), :] += block
    for s in range(2):
        for part in range(2):
            q = 2 * s + part
            gradient[s, part] = frame[q, HALO : HALO + N, 0:N] + REG_WEIGHT * obj[s, part]
            row_top[s, part] = frame[q, 0:HALO, 0:N]
            row_bottom[s, part] = frame[q, HALO + N : FRAME, 0:N]

        def strips(rows):
            re, im = frame[2 * s, rows, N:FRAME], frame[2 * s + 1, rows, N:FRAME]
            right = jnp.where(low, re, pltpu.roll(im, HALO, 1))
            left = jnp.where(low, pltpu.roll(re, HALO, 1), im)
            return right, left

        for rows in chunks(N, HALO):
            right, left = strips(slice(HALO + rows.start, HALO + rows.stop))
            col_right[s, rows] = right
            col_left[s, rows] = left
        right, left = strips(slice(HALO + N, FRAME))
        corner_right[s, 0:HALO] = right
        corner_left[s, 0:HALO] = left
        right, left = strips(slice(0, HALO))
        corner_right[s, HALO : 2 * HALO] = right
        corner_left[s, HALO : 2 * HALO] = left


def put_rows(out, first_row, sums):
    for k, value in enumerate(sums):
        out[first_row + k : first_row + k + 1, :] = jnp.sum(value, axis=0, keepdims=True)


def fold(value):
    rows = value.shape[0]
    value = value[:, : N // 2] + value[:, N // 2 :]
    return sum(value[r : r + 8] for r in range(0, rows, 8))


def accumulate(terms, count, out):
    def body(k, carry):
        rows = pl.ds((k % (N // 16)) * 16, 16)
        q = k // (N // 16)
        return tuple(a + fold(b) for a, b in zip(carry, terms(q // 2, q % 2, rows)))

    zero = tuple(jnp.zeros((8, N // 2), F32) for _ in range(count))
    put_rows(out, 0, lax.fori_loop(0, 4 * (N // 16), body, zero))


def sy_kernel(steps, changes, after, out):
    def terms(s, part, rows):
        st = [steps[i, s, part, rows, :].astype(F32) for i in range(MEM)]
        ch = [changes[i, s, part, rows, :].astype(F32) for i in range(MEM)]
        return [st[i] * ch[j] for i, j in SY_PAIRS]

    accumulate(terms, len(SY_PAIRS), out)


def yy_kernel(changes, after, out):
    def terms(s, part, rows):
        ch = [changes[i, s, part, rows, :].astype(F32) for i in range(MEM)]
        return [ch[i] * ch[j] for i, j in SY_PAIRS]

    accumulate(terms, len(SY_PAIRS), out)


def dots_kernel(gradient_in, row_up, row_down, col_left, col_right, steps, changes,
                gram_sy, gram_yy, gradient, out, stored, sums, sem):
    low = lanes((64, 2 * HALO)) < HALO
    for s in range(2):
        for part in range(2):
            for rows in chunks(N, 64):
                now = gradient_in[s, part, rows, :]
                if rows.start == 0:
                    now = now + row_up[s, part]
                if rows.stop == N:
                    now = now + row_down[s, part]
                a, b = col_left[s, rows], col_right[s, rows]
                if part == 0:
                    b = pltpu.roll(b, HALO, 1)
                else:
                    a = pltpu.roll(a, HALO, 1)
                gradient[s, part, rows, 0 : 2 * HALO] = now[:, : 2 * HALO] + jnp.where(low, a, 0.0)
                gradient[s, part, rows, N - 2 * HALO : N] = now[:, N - 2 * HALO :] + jnp.where(low, 0.0, b)
    copy = pltpu.make_async_copy(gradient, stored, sem)
    copy.start()

    def body(k, carry):
        q = k // (N // 64)
        rows = pl.ds((k % (N // 64)) * 64, 64)
        s, part = q // 2, q % 2
        g = gradient[s, part, rows, :]
        new = [fold(steps[i, s, part, rows, :].astype(F32) * g) for i in range(MEM)]
        new += [fold(changes[i, s, part, rows, :].astype(F32) * g) for i in range(MEM)]
        return tuple(a + b for a, b in zip(carry, new))

    zero = tuple(jnp.zeros((8, N // 2), F32) for _ in range(2 * MEM))
    sums[...] = jnp.zeros(sums.shape, F32)
    sums[0 : len(SY_PAIRS), :] = gram_sy[0 : len(SY_PAIRS), :]
    sums[len(SY_PAIRS) : SG_ROW, :] = gram_yy[0 : len(SY_PAIRS), :]
    put_rows(sums, SG_ROW, lax.fori_loop(0, 4 * (N // 64), body, zero))
    totals = jnp.sum(sums[...], axis=1, keepdims=True)
    row = lax.broadcasted_iota(jnp.int32, (128, 128), 0)
    spread = jnp.where(row == lanes((128, 128)), totals, 0.0)
    total_row = jnp.sum(spread, axis=0, keepdims=True)
    out[...] = jnp.broadcast_to(total_row[None], (128, 1, 128))
    copy.wait()


def final_kernel(parts, obj, gradient, steps, changes, out, result, sems):
    total = jnp.sum(parts[:, 0, :], axis=0, keepdims=True)
    row = lax.broadcasted_iota(jnp.int32, (128, 128), 0)
    diagonal = jnp.where(row == lanes((128, 128)), total, 0.0)
    splats = jnp.broadcast_to(jnp.sum(diagonal, axis=1, keepdims=True), (128, 128))

    def value(k):
        return splats[k : k + 1, :]

    sy = {pair: value(k) for pair, k in SY_ROW.items()}
    yy = {pair: value(k) for pair, k in YY_ROW.items()}
    inverse = [1.0 / sy[i, i] for i in range(MEM)]
    scaling = sy[MEM - 1, MEM - 1] / yy[MEM - 1, MEM - 1]
    alpha = [None] * MEM
    for i in reversed(range(MEM)):
        term = value(SG_ROW + i)
        for j in reversed(range(i + 1, MEM)):
            term = term - alpha[j] * sy[i, j]
        alpha[i] = term * inverse[i]
    weights = []
    for i in range(MEM):
        term = value(YG_ROW + i)
        for j in reversed(range(MEM)):
            term = term - alpha[j] * yy[min(i, j), max(i, j)]
        term = scaling * term
        for j in range(i):
            term = term + weights[j] * sy[j, i]
        weights.append(alpha[i] - term * inverse[i])

    def wide(x):
        return jnp.broadcast_to(jnp.concatenate([x, x], 1), (CHUNK, N))

    scale = wide(scaling)
    step_weights = [wide(w) for w in weights]
    change_weights = [wide(scaling * a) for a in alpha]
    copies = []
    for s in range(2):
        for part in range(2):

            def body(k, carry):
                rows = pl.ds(k * CHUNK, CHUNK)
                acc = scale * gradient[s, part, rows, :]
                for j in range(MEM):
                    acc = acc - change_weights[j] * changes[j, s, part, rows, :].astype(F32)
                    acc = acc + step_weights[j] * steps[j, s, part, rows, :].astype(F32)
                result[s, part, rows, :] = obj[s, part, rows, :] - acc
                return carry

            lax.fori_loop(0, N // CHUNK, body, 0)
            copies.append(pltpu.make_async_copy(result.at[s, part], out.at[s, part], sems.at[2 * s + part]))
            copies[-1].start()
    for copy in copies:
        copy.wait()


def shape(*dims, dtype=F32):
    return jax.ShapeDtypeStruct(dims, dtype)


def scratch(*dims, dtype=F32):
    return pltpu.VMEM(dims, dtype)


def call(kernel, outs, scratches, args, smem=0, raw=0, stored=()):
    return pl.pallas_call(
        kernel,
        out_shape=outs,
        in_specs=[SMEM] * smem + [ANY] * raw + [VMEM] * (len(args) - smem - raw),
        out_specs=tuple(ANY if k in stored else VMEM for k in range(len(outs))),
        scratch_shapes=scratches,
        compiler_params=PARAMS,
    )(*args)


def shifted(value, axis, step):
    size = lax.axis_size(axis)
    return lax.ppermute(value, axis, [(i, (i + step) % size) for i in range(size)])


def packed(value, columns):
    return jnp.concatenate([value[:, 0, :, columns], value[:, 1, :, columns]], -1)


def near_pairs(rows, modes):
    half = rows // modes
    pairs = []
    for t in range(rows):
        for m in range(modes):
            y = m * modes + t // half
            other = 2 * modes - 1 - y
            target = (other % modes) * half + t % half
            pairs.append((t * modes + m, target * modes + other // modes))
    return pairs


def per_device(object_field, probe, patterns, offsets, phase, past_steps, past_changes):
    rows_axis, modes_axis = lax.axis_size("ty"), lax.axis_size("mode")
    core = (lax.axis_index("ty") & 1).astype(jnp.int32).reshape(1)
    tables = dft_tables()
    first, last = slice(0, HALO), slice(N - HALO, N)
    strip, side, corner = shape(2, 2, HALO, N), shape(2, N, 2 * HALO), shape(2, 2 * HALO, 2 * HALO)
    row_first, row_last, col_first, col_last, chosen = call(
        pack_kernel, (strip, strip, side, side, shape(N, 2 * N)),
        [scratch(2, 2, N, 2 * HALO), scratch(2, 2, N, 2 * HALO), pltpu.SemaphoreType.DMA((5,))],
        (core, pltpu.with_memory_space_constraint(object_field, pltpu.HBM),
         pltpu.with_memory_space_constraint(probe, pltpu.HBM)), smem=1, raw=2)
    top = shifted(row_last, "ty", 1)
    bottom = shifted(row_first, "ty", -1)
    left = shifted(col_last, "tx", 1)
    right = shifted(col_first, "tx", -1)
    near = lax.ppermute(chosen, ("ty", "mode"), near_pairs(rows_axis, modes_axis))
    strips, phase = lax.optimization_barrier((jnp.concatenate([bottom, top], 2), phase))
    corner_last, corner_first = packed(strips, last), packed(strips, first)
    corner_left = shifted(corner_last, "tx", 1)
    corner_right = shifted(corner_first, "tx", -1)
    kernel = jnp.stack([jnp.cos(phase), jnp.sin(phase)])
    gram_sy = call(sy_kernel, (shape(16, 128),), [], (past_steps, past_changes, corner_first))[0]

    def work(slots):
        return [scratch(slots, N, 2 * N, dtype=BF16), scratch(slots, 2 * N, 2 * N, dtype=BF16),
                scratch(slots, N, 2 * N)]

    window, psi1, far, intensity = call(
        own_kernel,
        (shape(2, N, 2 * N), shape(2, N, 2 * N), shape(2, N, 2 * N), shape(N, N)),
        [scratch(4, FRAME + 8, FRAME)] + work(2),
        (offsets, object_field, top, bottom, left, right, corner_left, corner_right, probe, kernel,
         gram_sy) + tables,
        smem=1,
    )
    near, intensity = lax.optimization_barrier((near, intensity))
    swapped = lax.ppermute(near, "ty", [(i, i ^ 1) for i in range(rows_axis)])
    psi1_near, far_near, intensity_near = call(
        near_kernel, (shape(1, N, 2 * N), shape(1, N, 2 * N), shape(N, N)), work(1),
        (near, kernel) + tables + (window,))
    partial, row_top, row_bottom, col_left, col_right, corner_left, corner_right = call(
        other_kernel,
        (shape(2, 2, N, N), strip, strip, side, side, corner, corner),
        [scratch(1, N, 2 * N), scratch(1, N, 2 * N), scratch(N, N)] + work(4)
        + [scratch(2, 2, N, 2 * N), scratch(4, FRAME + 8, FRAME)],
        (offsets, object_field, probe, near, swapped, kernel) + tables
        + (patterns, window, psi1, far, intensity, psi1_near, far_near, intensity_near),
        smem=1,
    )
    from_left = shifted(corner_right, "tx", 1)
    from_right = shifted(corner_left, "tx", -1)
    side_left = shifted(col_right, "tx", 1)
    side_right = shifted(col_left, "tx", -1)


    def with_corners(strip_now, rows):
        def unpacked(block):
            return jnp.stack([block[:, rows, :HALO], block[:, rows, HALO:]], 1)

        gap = jnp.zeros(strip_now.shape[:3] + (N - 2 * HALO,), F32)
        return strip_now + jnp.concatenate([unpacked(from_left), gap, unpacked(from_right)], -1)

    below, above = with_corners(row_bottom, slice(0, HALO)), with_corners(row_top, slice(HALO, 2 * HALO))
    row_up = shifted(below, "ty", 1)
    row_down = shifted(above, "ty", -1)
    gram_yy = call(yy_kernel, (shape(16, 128),), [], (past_changes, above))[0]
    gradient, sums, stored = call(
        dots_kernel,
        (shape(2, 2, N, N), shape(128, 1, 128), shape(2, 2, N, N)),
        [scratch(128, 128), pltpu.SemaphoreType.DMA],
        (partial, row_up, row_down, side_left, side_right, past_steps, past_changes,
         gram_sy, gram_yy),
        stored=(2,),
    )
    parts = lax.all_to_all(sums, TILES, 0, 0)
    new_object = call(
        final_kernel, (shape(2, 2, N, N),), [scratch(2, 2, N, N), pltpu.SemaphoreType.DMA((4,))],
        (parts, object_field, gradient, past_steps, past_changes), stored=(0,))[0]
    return (new_object, stored)


def solution(mesh):
    placed = (
        P(None, None, "ty", "tx"),
        P("mode", None, None),
        P(TILES, None, None),
        P(TILES, None),
        P(),
        P(None, None, None, "ty", "tx"),
        P(None, None, None, "ty", "tx"),
    )
    return jax.shard_map(
        per_device,
        mesh=mesh,
        in_specs=placed,
        out_specs=(P(None, None, "ty", "tx"), P(None, None, "ty", "tx")),
        check_vma=False,
    )
```

```python
import math

import jax
import jax.numpy as jnp
import numpy as np
from jax import lax
from jax.experimental import pallas as pl
from jax.experimental.pallas import tpu as pltpu
from jax.sharding import PartitionSpec as P

MODES = 4
HALO = 64
REG_WEIGHT = 1.0
N = 256
FRAME = N + 2 * HALO
MEM = 5
CHUNK = 32
F32 = jnp.float32
BF16 = jnp.bfloat16
TILES = ("ty", "tx")
VMEM = pl.BlockSpec(memory_space=pltpu.VMEM)
ANY = pl.BlockSpec(memory_space=pltpu.HBM)
SMEM = pl.BlockSpec(memory_space=pltpu.SMEM)
PARAMS = pltpu.CompilerParams(vmem_limit_bytes=40 * 1024 * 1024)
SY_PAIRS = [(i, j) for i in range(MEM) for j in range(i, MEM)]
SY_ROW = {pair: k for k, pair in enumerate(SY_PAIRS)}
YY_ROW = {pair: len(SY_PAIRS) + k for k, pair in enumerate(SY_PAIRS)}
SG_ROW = 2 * len(SY_PAIRS)
YG_ROW = SG_ROW + MEM
ROWS = YG_ROW + MEM


def dft_tables():
    indices = np.arange(N, dtype=np.int32)
    products = indices[:, None] * indices[None, :] % N
    angles = products.astype(np.float32) * np.float32(2.0 * math.pi / N)
    cosine = (np.cos(angles) / np.float32(math.sqrt(N))).astype(np.float32)
    sine = (np.sin(angles) / np.float32(math.sqrt(N))).astype(np.float32)
    forward = np.block([[cosine, -sine], [sine, cosine]])
    inverse = np.block([[cosine, sine], [-sine, cosine]])
    left = np.concatenate([cosine, sine], 1)
    return tuple(jnp.asarray(t, BF16) for t in (forward, inverse, left))


def lanes(shape):
    return lax.broadcasted_iota(jnp.int32, shape, len(shape) - 1)


def chunks(total=N, step=CHUNK):
    return [slice(c, c + step) for c in range(0, total, step)]


def aligned(offset):
    base = pl.multiple_of((offset // 8) * 8, 8)
    return base, offset - base


def product(a, b, conjugate):
    ar, ai = a
    br, bi = b
    if conjugate:
        return ar * br + ai * bi, ar * bi - ai * br
    return ar * br - ai * bi, ar * bi + ai * br


def halves(ref, index, rows):
    return ref[index, rows, 0:N], ref[index, rows, N : 2 * N]


def first_pass(xb, ks, m, right, inverse):
    y = jnp.dot(xb[m], right[...], preferred_element_type=F32).astype(BF16)
    yr, yi = y[:, :N], y[:, N:]
    ks[m, 0:N, :] = y
    if inverse:
        ks[m, N : 2 * N, 0:N] = -yi
        ks[m, N : 2 * N, N : 2 * N] = yr
    else:
        ks[m, N : 2 * N, 0:N] = yi
        ks[m, N : 2 * N, N : 2 * N] = -yr


def second_pass(ks, m, left):
    return jnp.dot(left[...], ks[m], preferred_element_type=F32)


def propagate(xb, ks, zs, m, kernel, tables, adjoint):
    forward, inverse, left = tables
    first_pass(xb, ks, m, forward, False)
    yield
    zs[m] = second_pass(ks, m, left)
    yield
    for rows in chunks():
        h = (kernel[0, rows, :], kernel[1, rows, :])
        re, im = product(h, halves(zs, m, rows), adjoint)
        xb[m, rows, 0:N] = re.astype(BF16)
        xb[m, rows, N : 2 * N] = im.astype(BF16)
    yield
    first_pass(xb, ks, m, inverse, True)
    yield


def enter_mode(slot, psi0, psi1, window, kernel, tables, xb, ks, zs):
    for rows in chunks():
        re, im = product(halves(window, 0, rows), (psi0[rows, 0:N], psi0[rows, N : 2 * N]), False)
        xb[slot, rows, 0:N] = re.astype(BF16)
        xb[slot, rows, N : 2 * N] = im.astype(BF16)
    yield
    yield from propagate(xb, ks, zs, slot, kernel, tables, False)
    psi1[...] = second_pass(ks, slot, tables[2])
    yield


def leave_mode(slot, psi1, far, window, tables, xb, ks):
    for rows in chunks():
        re, im = product(halves(window, 1, rows), (psi1[rows, 0:N], psi1[rows, N : 2 * N]), False)
        xb[slot, rows, 0:N] = re.astype(BF16)
        xb[slot, rows, N : 2 * N] = im.astype(BF16)
    yield
    first_pass(xb, ks, slot, tables[0], False)
    yield
    far[...] = second_pass(ks, slot, tables[2])
    yield


def chain(*tasks):
    for task in tasks:
        yield from task


def together(tasks):
    tasks = list(tasks)
    while tasks:
        tasks = [task for task in tasks if next(task, tasks) is not tasks]
        if tasks:
            yield


def backward_mode(slot, psi0, psi1, far, scale, window, kernel, tables, pieces, xb, ks, zs):
    forward, inverse, left = tables
    pair, m = divmod(slot, 2)
    k = slot

    def collect(s, rows, re, im):
        if m:
            re, im = re + pieces[pair, s, rows, 0:N], im + pieces[pair, s, rows, N : 2 * N]
        pieces[pair, s, rows, 0:N] = re
        pieces[pair, s, rows, N : 2 * N] = im

    for rows in chunks():
        factor = scale[rows, :]
        re, im = (far[rows, 0:N], far[rows, N : 2 * N])
        xb[k, rows, 0:N] = (factor * re).astype(BF16)
        xb[k, rows, N : 2 * N] = (factor * im).astype(BF16)
    yield
    first_pass(xb, ks, k, inverse, True)
    yield
    zs[k] = second_pass(ks, k, left)
    yield
    for rows in chunks():
        current = halves(zs, k, rows)
        collect(1, rows, *product((psi1[rows, 0:N], psi1[rows, N : 2 * N]), current, True))
        re, im = product(halves(window, 1, rows), current, True)
        xb[k, rows, 0:N] = re.astype(BF16)
        xb[k, rows, N : 2 * N] = im.astype(BF16)
    yield
    yield from propagate(xb, ks, zs, k, kernel, tables, True)
    zs[k] = second_pass(ks, k, left)
    yield
    for rows in chunks():
        collect(0, rows, *product((psi0[rows, 0:N], psi0[rows, N : 2 * N]), halves(zs, k, rows), True))
    yield


def interleave(tasks):
    waiting, running = list(tasks), []
    while waiting or running:
        if waiting:
            running.append(waiting.pop(0))
        running = [task for task in running if next(task, running) is not running]


def pack_kernel(core, obj, probe, row_first, row_last, col_first, col_last, chosen, edge_first, edge_last, sems):
    low = lanes((N, 2 * HALO)) < HALO
    moves = [
        (obj.at[:, :, :, 0 : 2 * HALO], edge_first),
        (obj.at[:, :, :, N - 2 * HALO : N], edge_last),
        (obj.at[:, :, 0:HALO, :], row_first),
        (obj.at[:, :, N - HALO : N, :], row_last),
        (probe.at[core[0]], chosen),
    ]
    copies = [pltpu.make_async_copy(src, dst, sems.at[k]) for k, (src, dst) in enumerate(moves)]
    for copy in copies:
        copy.start()
    copies[0].wait()
    for s in range(2):
        col_first[s] = jnp.where(low, edge_first[s, 0], pltpu.roll(edge_first[s, 1], HALO, 1))
    copies[1].wait()
    for s in range(2):
        col_last[s] = jnp.where(low, pltpu.roll(edge_last[s, 0], HALO, 1), edge_last[s, 1])
    for copy in copies[2:]:
        copy.wait()


def own_kernel(offsets, obj, top, bottom, left_in, right_in, corner_up, corner_down, probe, kernel,
               fwd_t, inv_t, left_t, window, psi1, ext, xb, ks, zs):
    tables = (fwd_t, inv_t, left_t)
    low = lanes((HALO, 2 * HALO)) < HALO

    def border(right_block, left_block, part):
        if part == 0:
            return jnp.where(low, right_block, pltpu.roll(left_block, HALO, 1))
        return jnp.where(low, pltpu.roll(right_block, HALO, 1), left_block)

    row_base, row_rest = aligned(offsets[0, 0])
    shift = lax.rem(HALO + FRAME - offsets[0, 1], FRAME)
    for s in range(2):
        for part in range(2):
            q = 2 * s + part
            ext[q, 0:HALO, 0:N] = top[s, part]
            ext[q, HALO : HALO + N, 0:N] = obj[s, part]
            ext[q, HALO + N : FRAME, 0:N] = bottom[s, part]
            ext[q, 0:HALO, N:FRAME] = border(
                corner_up[s, 1], corner_up[s, 0], part)
            ext[q, HALO + N : FRAME, N:FRAME] = border(
                corner_down[s, 1], corner_down[s, 0], part)
            for rows in chunks(N, HALO):
                ext[q, HALO + rows.start : HALO + rows.stop, N:FRAME] = border(
                    right_in[s, rows], left_in[s, rows], part)
            for rows in chunks(N, 64):
                block = ext[q, pl.ds(row_base + rows.start, 72), :]
                block = pltpu.roll(block, lax.rem(72 - row_rest, 72), 0)[:64]
                window[s, rows, part * N : (part + 1) * N] = pltpu.roll(block, shift, 1)[:, :N]
    interleave([together(
        enter_mode(m, probe.at[m], psi1.at[m], window, kernel, tables, xb, ks, zs) for m in range(2))])


def other_kernel(offsets, obj, probe, near, swapped, kernel, fwd_t, inv_t, left_t, patterns, window, psi1_own,
                 gradient, row_top, row_bottom, col_left, col_right, corner_left, corner_right,
                 psi1, far, inten, xb, ks, zs, back, frame):
    tables = (fwd_t, inv_t, left_t)
    entering = [(probe.at[0], psi1_own.at[0]), (probe.at[1], psi1_own.at[1]), (near, psi1.at[0]), (swapped, psi1.at[1])]

    def leaving(k):
        return leave_mode(k, entering[k][1], far.at[k], window, tables, xb, ks)

    interleave([
        together(
            chain(enter_mode(k, *entering[k], window, kernel, tables, xb, ks, zs), leaving(k)) for k in (2, 3)),
        together(leaving(k) for k in (0, 1)),
    ])
    for rows in chunks():
        terms = []
        for k in range(4):
            re, im = halves(far, k, rows)
            terms.append(re * re + im * im)
        inten[rows, :] = (terms[0] + terms[1]) + (terms[2] + terms[3])
    for rows in chunks():
        inten[rows, :] = (inten[rows, :] * (1.0 / MODES) - patterns[0, rows, :]) * (2.0 / MODES)
    row_base, row_rest = aligned(offsets[0, 0])
    shift = lax.rem(HALO + N + offsets[0, 1], FRAME)
    interleave(
        together(
            backward_mode(k, *entering[k], far.at[k], inten, window, kernel, tables, back, xb, ks, zs) for k in pair)
        for pair in ((0, 1), (2, 3)))
    low = lanes((HALO, 2 * HALO)) < HALO
    zero = jnp.zeros((HALO, 2 * HALO), F32)
    gap = jnp.zeros((8, FRAME), F32)
    frame[...] = jnp.zeros(frame.shape, F32)
    for q in range(4):
        s, part = divmod(q, 2)
        for rows in chunks(N, 64):
            columns = slice(part * N, (part + 1) * N)
            block = back[0, s, rows, columns] + back[1, s, rows, columns]
            block = pltpu.roll(jnp.concatenate([block, zero], 1), shift, 1)
            block = pltpu.roll(jnp.concatenate([block, gap], 0), row_rest, 0)
            frame[q, pl.ds(row_base + rows.start, 72), :] += block
    for s in range(2):
        for part in range(2):
            q = 2 * s + part
            gradient[s, part] = frame[q, HALO : HALO + N, 0:N] + REG_WEIGHT * obj[s, part]
            row_top[s, part] = frame[q, 0:HALO, 0:N]
            row_bottom[s, part] = frame[q, HALO + N : FRAME, 0:N]

        def strips(rows):
            re, im = frame[2 * s, rows, N:FRAME], frame[2 * s + 1, rows, N:FRAME]
            right = jnp.where(low, re, pltpu.roll(im, HALO, 1))
            left = jnp.where(low, pltpu.roll(re, HALO, 1), im)
            return right, left

        for rows in chunks(N, HALO):
            right, left = strips(slice(HALO + rows.start, HALO + rows.stop))
            col_right[s, rows] = right
            col_left[s, rows] = left
        corner_right[s, 0], corner_left[s, 0] = strips(slice(HALO + N, FRAME))
        corner_right[s, 1], corner_left[s, 1] = strips(slice(0, HALO))


def put_rows(out, first_row, sums):
    for k, value in enumerate(sums):
        out[first_row + k : first_row + k + 1, :] = jnp.sum(value, axis=0, keepdims=True)


def fold(value):
    rows = value.shape[0]
    value = value[:, : N // 2] + value[:, N // 2 :]
    return sum(value[r : r + 8] for r in range(0, rows, 8))


def accumulate(terms, count, out):
    def body(k, carry):
        rows = pl.ds((k % (N // 16)) * 16, 16)
        q = k // (N // 16)
        return tuple(a + fold(b) for a, b in zip(carry, terms(q // 2, q % 2, rows)))

    zero = tuple(jnp.zeros((8, N // 2), F32) for _ in range(count))
    put_rows(out, 0, lax.fori_loop(0, 4 * (N // 16), body, zero))


def gram_kernel(steps, changes, after, out):
    def terms(s, part, rows):
        st = [steps[i, s, part, rows, :].astype(F32) for i in range(MEM)]
        ch = [changes[i, s, part, rows, :].astype(F32) for i in range(MEM)]
        return [st[i] * ch[j] for i, j in SY_PAIRS] + [ch[i] * ch[j] for i, j in SY_PAIRS]

    accumulate(terms, 2 * len(SY_PAIRS), out)


def dots_kernel(gradient_in, row_up, row_down, col_left, col_right, steps, changes,
                gram, gradient, out, stored, sums, sem):
    low = lanes((64, 2 * HALO)) < HALO
    for s in range(2):
        for part in range(2):
            for rows in chunks(N, 64):
                now = gradient_in[s, part, rows, :]
                if rows.start == 0:
                    now = now + row_up[s, part]
                if rows.stop == N:
                    now = now + row_down[s, part]
                a, b = col_left[s, rows], col_right[s, rows]
                if part == 0:
                    b = pltpu.roll(b, HALO, 1)
                else:
                    a = pltpu.roll(a, HALO, 1)
                gradient[s, part, rows, 0 : 2 * HALO] = now[:, : 2 * HALO] + jnp.where(low, a, 0.0)
                gradient[s, part, rows, N - 2 * HALO : N] = now[:, N - 2 * HALO :] + jnp.where(low, 0.0, b)
    copy = pltpu.make_async_copy(gradient, stored, sem)
    copy.start()

    def body(k, carry):
        q = k // (N // 64)
        rows = pl.ds((k % (N // 64)) * 64, 64)
        s, part = q // 2, q % 2
        g = gradient[s, part, rows, :]
        new = [fold(steps[i, s, part, rows, :].astype(F32) * g) for i in range(MEM)]
        new += [fold(changes[i, s, part, rows, :].astype(F32) * g) for i in range(MEM)]
        return tuple(a + b for a, b in zip(carry, new))

    zero = tuple(jnp.zeros((8, N // 2), F32) for _ in range(2 * MEM))
    sums[...] = jnp.zeros(sums.shape, F32)
    sums[0:SG_ROW, :] = gram[0:SG_ROW, :]
    put_rows(sums, SG_ROW, lax.fori_loop(0, 4 * (N // 64), body, zero))
    totals = jnp.sum(sums[...], axis=1, keepdims=True)
    row = lax.broadcasted_iota(jnp.int32, (128, 128), 0)
    spread = jnp.where(row == lanes((128, 128)), totals, 0.0)
    total_row = jnp.sum(spread, axis=0, keepdims=True)
    out[...] = jnp.broadcast_to(total_row[None], (128, 1, 128))
    copy.wait()


def final_kernel(parts, obj, gradient, steps, changes, out, result, sems):
    total = jnp.sum(parts[:, 0, :], axis=0, keepdims=True)
    row = lax.broadcasted_iota(jnp.int32, (128, 128), 0)
    diagonal = jnp.where(row == lanes((128, 128)), total, 0.0)
    splats = jnp.broadcast_to(jnp.sum(diagonal, axis=1, keepdims=True), (128, 128))

    def value(k):
        return splats[k : k + 1, :]

    sy = {pair: value(k) for pair, k in SY_ROW.items()}
    yy = {pair: value(k) for pair, k in YY_ROW.items()}
    inverse = [1.0 / sy[i, i] for i in range(MEM)]
    scaling = sy[MEM - 1, MEM - 1] / yy[MEM - 1, MEM - 1]
    alpha = [None] * MEM
    for i in reversed(range(MEM)):
        term = value(SG_ROW + i)
        for j in reversed(range(i + 1, MEM)):
            term = term - alpha[j] * sy[i, j]
        alpha[i] = term * inverse[i]
    weights = []
    for i in range(MEM):
        term = value(YG_ROW + i)
        for j in reversed(range(MEM)):
            term = term - alpha[j] * yy[min(i, j), max(i, j)]
        term = scaling * term
        for j in range(i):
            term = term + weights[j] * sy[j, i]
        weights.append(alpha[i] - term * inverse[i])

    def wide(x):
        return jnp.broadcast_to(jnp.concatenate([x, x], 1), (CHUNK, N))

    scale = wide(scaling)
    step_weights = [wide(w) for w in weights]
    change_weights = [wide(scaling * a) for a in alpha]
    copies = []
    for s in range(2):
        for part in range(2):

            def body(k, carry):
                rows = pl.ds(k * CHUNK, CHUNK)
                acc = scale * gradient[s, part, rows, :]
                for j in range(MEM):
                    acc = acc - change_weights[j] * changes[j, s, part, rows, :].astype(F32)
                    acc = acc + step_weights[j] * steps[j, s, part, rows, :].astype(F32)
                result[s, part, rows, :] = obj[s, part, rows, :] - acc
                return carry

            lax.fori_loop(0, N // CHUNK, body, 0)
            copies.append(pltpu.make_async_copy(result.at[s, part], out.at[s, part], sems.at[2 * s + part]))
            copies[-1].start()
    for copy in copies:
        copy.wait()


def shape(*dims, dtype=F32):
    return jax.ShapeDtypeStruct(dims, dtype)


def scratch(*dims, dtype=F32):
    return pltpu.VMEM(dims, dtype)


def call(kernel, outs, scratches, args, smem=0, raw=0, stored=()):
    return pl.pallas_call(
        kernel,
        out_shape=outs,
        in_specs=[SMEM] * smem + [ANY] * raw + [VMEM] * (len(args) - smem - raw),
        out_specs=tuple(ANY if k in stored else VMEM for k in range(len(outs))),
        scratch_shapes=scratches,
        compiler_params=PARAMS,
    )(*args)


def shifted(value, axis, step):
    size = lax.axis_size(axis)
    return lax.ppermute(value, axis, [(i, (i + step) % size) for i in range(size)])


def near_pairs(rows, modes):
    half = rows // modes
    pairs = []
    for t in range(rows):
        for m in range(modes):
            y = m * modes + t // half
            other = 2 * modes - 1 - y
            target = (other % modes) * half + t % half
            pairs.append((t * modes + m, target * modes + other // modes))
    return pairs


def per_device(object_field, probe, patterns, offsets, phase, past_steps, past_changes):
    rows_axis, modes_axis = lax.axis_size("ty"), lax.axis_size("mode")
    core = (lax.axis_index("ty") & 1).astype(jnp.int32).reshape(1)
    tables = dft_tables()
    first, last = slice(0, HALO), slice(N - HALO, N)
    strip, side, corner = shape(2, 2, HALO, N), shape(2, N, 2 * HALO), shape(2, 2, HALO, 2 * HALO)
    row_first, row_last, col_first, col_last, chosen = call(
        pack_kernel, (strip, strip, side, side, shape(N, 2 * N)),
        [scratch(2, 2, N, 2 * HALO), scratch(2, 2, N, 2 * HALO), pltpu.SemaphoreType.DMA((5,))],
        (core, pltpu.with_memory_space_constraint(object_field, pltpu.HBM),
         pltpu.with_memory_space_constraint(probe, pltpu.HBM)), smem=1, raw=2)
    top = shifted(row_last, "ty", 1)
    bottom = shifted(row_first, "ty", -1)
    left = shifted(col_last, "tx", 1)
    right = shifted(col_first, "tx", -1)
    near = lax.ppermute(chosen, ("ty", "mode"), near_pairs(rows_axis, modes_axis))
    sides = jnp.stack([left, right], 1)
    going_down, going_up = sides[:, :, last], sides[:, :, first]
    corner_up = shifted(going_down, "ty", 1)
    corner_down = shifted(going_up, "ty", -1)
    kernel = jnp.stack([jnp.cos(phase), jnp.sin(phase)])
    near, top, bottom, corner_up, corner_down, kernel = lax.optimization_barrier(
        (near, top, bottom, corner_up, corner_down, kernel))
    swapped = lax.ppermute(near, "ty", [(i, i ^ 1) for i in range(rows_axis)])

    def work(slots):
        return [scratch(slots, N, 2 * N, dtype=BF16), scratch(slots, 2 * N, 2 * N, dtype=BF16),
                scratch(slots, N, 2 * N)]

    window, psi1 = call(
        own_kernel,
        (shape(2, N, 2 * N), shape(2, N, 2 * N)),
        [scratch(4, FRAME + 8, FRAME)] + work(2),
        (offsets, object_field, top, bottom, left, right, corner_up, corner_down, probe, kernel)
        + tables,
        smem=1,
    )
    partial, row_top, row_bottom, col_left, col_right, corner_left, corner_right = call(
        other_kernel,
        (shape(2, 2, N, N), strip, strip, side, side, corner, corner),
        [scratch(2, N, 2 * N), scratch(4, N, 2 * N), scratch(N, N)] + work(4)
        + [scratch(2, 2, N, 2 * N), scratch(4, FRAME + 8, FRAME)],
        (offsets, object_field, probe, near, swapped, kernel) + tables
        + (patterns, window, psi1),
        smem=1,
    )
    from_left = shifted(corner_right, "tx", 1)
    from_right = shifted(corner_left, "tx", -1)
    side_left = shifted(col_right, "tx", 1)
    side_right = shifted(col_left, "tx", -1)

    def with_corners(strip_now, k):
        def unpacked(block):
            return jnp.stack([block[:, k, :, :HALO], block[:, k, :, HALO:]], 1)

        gap = jnp.zeros(strip_now.shape[:3] + (N - 2 * HALO,), F32)
        return strip_now + jnp.concatenate([unpacked(from_left), gap, unpacked(from_right)], -1)

    below, above = with_corners(row_bottom, 0), with_corners(row_top, 1)
    row_up = shifted(below, "ty", 1)
    row_down = shifted(above, "ty", -1)
    gram = call(gram_kernel, (shape(32, 128),), [], (past_steps, past_changes, above))[0]
    gradient, sums, stored = call(
        dots_kernel,
        (shape(2, 2, N, N), shape(128, 1, 128), shape(2, 2, N, N)),
        [scratch(128, 128), pltpu.SemaphoreType.DMA],
        (partial, row_up, row_down, side_left, side_right, past_steps, past_changes,
         gram),
        stored=(2,),
    )
    parts = lax.all_to_all(sums, TILES, 0, 0)
    new_object = call(
        final_kernel, (shape(2, 2, N, N),), [scratch(2, 2, N, N), pltpu.SemaphoreType.DMA((4,))],
        (parts, object_field, gradient, past_steps, past_changes), stored=(0,))[0]
    return (new_object, stored)


def solution(mesh):
    placed = (
        P(None, None, "ty", "tx"),
        P("mode", None, None),
        P(TILES, None, None),
        P(TILES, None),
        P(),
        P(None, None, None, "ty", "tx"),
        P(None, None, None, "ty", "tx"),
    )
    return jax.shard_map(
        per_device,
        mesh=mesh,
        in_specs=placed,
        out_specs=(P(None, None, "ty", "tx"), P(None, None, "ty", "tx")),
        check_vma=False,
    )
```

```python
import math

import jax
import jax.numpy as jnp
import numpy as np
from jax import lax
from jax.experimental import pallas as pl
from jax.experimental.pallas import tpu as pltpu
from jax.sharding import PartitionSpec as P

MODES = 4
HALO = 64
REG_WEIGHT = 1.0
N = 256
FRAME = N + 2 * HALO
MEM = 5
CHUNK = 32
F32 = jnp.float32
BF16 = jnp.bfloat16
TILES = ("ty", "tx")
VMEM = pl.BlockSpec(memory_space=pltpu.VMEM)
ANY = pl.BlockSpec(memory_space=pltpu.HBM)
SMEM = pl.BlockSpec(memory_space=pltpu.SMEM)
PARAMS = pltpu.CompilerParams(vmem_limit_bytes=40 * 1024 * 1024)
SY_PAIRS = [(i, j) for i in range(MEM) for j in range(i, MEM)]
SY_ROW = {pair: k for k, pair in enumerate(SY_PAIRS)}
YY_ROW = {pair: len(SY_PAIRS) + k for k, pair in enumerate(SY_PAIRS)}
SG_ROW = 2 * len(SY_PAIRS)
YG_ROW = SG_ROW + MEM
ROWS = YG_ROW + MEM


def dft_tables():
    indices = np.arange(N, dtype=np.int32)
    products = indices[:, None] * indices[None, :] % N
    angles = products.astype(np.float32) * np.float32(2.0 * math.pi / N)
    cosine = (np.cos(angles) / np.float32(math.sqrt(N))).astype(np.float32)
    sine = (np.sin(angles) / np.float32(math.sqrt(N))).astype(np.float32)
    forward = np.block([[cosine, -sine], [sine, cosine]])
    inverse = np.block([[cosine, sine], [-sine, cosine]])
    left = np.concatenate([cosine, sine], 1)
    return tuple(jnp.asarray(t, BF16) for t in (forward, inverse, left))


def lanes(shape):
    return lax.broadcasted_iota(jnp.int32, shape, len(shape) - 1)


def chunks(total=N, step=CHUNK):
    return [slice(c, c + step) for c in range(0, total, step)]


def aligned(offset):
    base = pl.multiple_of((offset // 8) * 8, 8)
    return base, offset - base


def product(a, b, conjugate):
    ar, ai = a
    br, bi = b
    if conjugate:
        return ar * br + ai * bi, ar * bi - ai * br
    return ar * br - ai * bi, ar * bi + ai * br


def halves(ref, index, rows):
    return ref[index, rows, 0:N], ref[index, rows, N : 2 * N]


def first_pass(xb, ks, m, right, inverse):
    y = jnp.dot(xb[m], right[...], preferred_element_type=F32).astype(BF16)
    yr, yi = y[:, :N], y[:, N:]
    ks[m, 0:N, :] = y
    if inverse:
        ks[m, N : 2 * N, 0:N] = -yi
        ks[m, N : 2 * N, N : 2 * N] = yr
    else:
        ks[m, N : 2 * N, 0:N] = yi
        ks[m, N : 2 * N, N : 2 * N] = -yr


def second_pass(ks, m, left):
    return jnp.dot(left[...], ks[m], preferred_element_type=F32)


def propagate(xb, ks, zs, m, kernel, tables, adjoint):
    forward, inverse, left = tables
    first_pass(xb, ks, m, forward, False)
    yield
    zs[m] = second_pass(ks, m, left)
    yield
    for rows in chunks():
        h = (kernel[0, rows, :], kernel[1, rows, :])
        re, im = product(h, halves(zs, m, rows), adjoint)
        xb[m, rows, 0:N] = re.astype(BF16)
        xb[m, rows, N : 2 * N] = im.astype(BF16)
    yield
    first_pass(xb, ks, m, inverse, True)
    yield


def enter_mode(slot, psi0, psi1, window, kernel, tables, xb, ks, zs):
    for rows in chunks():
        re, im = product(halves(window, 0, rows), (psi0[rows, 0:N], psi0[rows, N : 2 * N]), False)
        xb[slot, rows, 0:N] = re.astype(BF16)
        xb[slot, rows, N : 2 * N] = im.astype(BF16)
    yield
    yield from propagate(xb, ks, zs, slot, kernel, tables, False)
    psi1[...] = second_pass(ks, slot, tables[2])
    yield


def leave_mode(slot, psi1, far, window, tables, xb, ks):
    for rows in chunks():
        re, im = product(halves(window, 1, rows), (psi1[rows, 0:N], psi1[rows, N : 2 * N]), False)
        xb[slot, rows, 0:N] = re.astype(BF16)
        xb[slot, rows, N : 2 * N] = im.astype(BF16)
    yield
    first_pass(xb, ks, slot, tables[0], False)
    yield
    far[...] = second_pass(ks, slot, tables[2])
    yield


def chain(*tasks):
    for task in tasks:
        yield from task


def together(tasks):
    tasks = list(tasks)
    while tasks:
        tasks = [task for task in tasks if next(task, tasks) is not tasks]
        if tasks:
            yield


def backward_mode(slot, psi0, psi1, far, scale, window, kernel, tables, pieces, xb, ks, zs):
    forward, inverse, left = tables
    pair, m = divmod(slot, 2)
    k = slot

    def collect(s, rows, re, im):
        if m:
            re, im = re + pieces[pair, s, rows, 0:N], im + pieces[pair, s, rows, N : 2 * N]
        pieces[pair, s, rows, 0:N] = re
        pieces[pair, s, rows, N : 2 * N] = im

    for rows in chunks():
        factor = scale[rows, :]
        re, im = (far[rows, 0:N], far[rows, N : 2 * N])
        xb[k, rows, 0:N] = (factor * re).astype(BF16)
        xb[k, rows, N : 2 * N] = (factor * im).astype(BF16)
    yield
    first_pass(xb, ks, k, inverse, True)
    yield
    zs[k] = second_pass(ks, k, left)
    yield
    for rows in chunks():
        current = halves(zs, k, rows)
        collect(1, rows, *product((psi1[rows, 0:N], psi1[rows, N : 2 * N]), current, True))
        re, im = product(halves(window, 1, rows), current, True)
        xb[k, rows, 0:N] = re.astype(BF16)
        xb[k, rows, N : 2 * N] = im.astype(BF16)
    yield
    yield from propagate(xb, ks, zs, k, kernel, tables, True)
    zs[k] = second_pass(ks, k, left)
    yield
    for rows in chunks():
        collect(0, rows, *product((psi0[rows, 0:N], psi0[rows, N : 2 * N]), halves(zs, k, rows), True))
    yield


def interleave(tasks):
    waiting, running = list(tasks), []
    while waiting or running:
        if waiting:
            running.append(waiting.pop(0))
        running = [task for task in running if next(task, running) is not running]


def pack_kernel(core, obj, probe, row_first, row_last, col_first, col_last, chosen, edge_first, edge_last, sems):
    low = lanes((N, 2 * HALO)) < HALO
    moves = [
        (obj.at[:, :, :, 0 : 2 * HALO], edge_first),
        (obj.at[:, :, :, N - 2 * HALO : N], edge_last),
        (obj.at[:, :, 0:HALO, :], row_first),
        (obj.at[:, :, N - HALO : N, :], row_last),
        (probe.at[core[0]], chosen),
    ]
    copies = [pltpu.make_async_copy(src, dst, sems.at[k]) for k, (src, dst) in enumerate(moves)]
    for copy in copies:
        copy.start()
    copies[0].wait()
    for s in range(2):
        col_first[s] = jnp.where(low, edge_first[s, 0], pltpu.roll(edge_first[s, 1], HALO, 1))
    copies[1].wait()
    for s in range(2):
        col_last[s] = jnp.where(low, pltpu.roll(edge_last[s, 0], HALO, 1), edge_last[s, 1])
    for copy in copies[2:]:
        copy.wait()


def border(right_block, left_block, part):
    low = lanes(right_block.shape) < HALO
    if part == 0:
        return jnp.where(low, right_block, pltpu.roll(left_block, HALO, 1))
    return jnp.where(low, pltpu.roll(right_block, HALO, 1), left_block)


def frame_kernel(obj, top, bottom, left_in, right_in, ext, clear):
    clear[...] = jnp.zeros(clear.shape, F32)
    for s in range(2):
        for part in range(2):
            q = 2 * s + part
            ext[q, 0:HALO, 0:N] = top[s, part]
            ext[q, HALO : HALO + N, 0:N] = obj[s, part]
            ext[q, HALO + N : FRAME, 0:N] = bottom[s, part]
            ext[q, FRAME : FRAME + 8, :] = jnp.zeros((8, FRAME), F32)
            for rows in chunks(N, HALO):
                ext[q, HALO + rows.start : HALO + rows.stop, N:FRAME] = border(
                    right_in[s, rows], left_in[s, rows], part)


def own_kernel(offsets, ext_in, corner_up, corner_down, probe, kernel, fwd_t, inv_t, left_t,
               window, psi1, ext, xb, ks, zs):
    tables = (fwd_t, inv_t, left_t)
    row_base, row_rest = aligned(offsets[0, 0])
    shift = lax.rem(HALO + FRAME - offsets[0, 1], FRAME)
    for s in range(2):
        for part in range(2):
            q = 2 * s + part
            ext[q, 0:HALO, N:FRAME] = border(corner_up[s, 1], corner_up[s, 0], part)
            ext[q, HALO + N : FRAME, N:FRAME] = border(corner_down[s, 1], corner_down[s, 0], part)
            for rows in chunks(N, 64):
                block = ext[q, pl.ds(row_base + rows.start, 72), :]
                block = pltpu.roll(block, lax.rem(72 - row_rest, 72), 0)[:64]
                window[s, rows, part * N : (part + 1) * N] = pltpu.roll(block, shift, 1)[:, :N]
    interleave([together(
        enter_mode(m, probe.at[m], psi1.at[m], window, kernel, tables, xb, ks, zs) for m in range(2))])


def other_kernel(offsets, obj, probe, near, swapped, kernel, fwd_t, inv_t, left_t, patterns, window, psi1_own, clear,
                 gradient, row_top, row_bottom, col_left, col_right, corner_left, corner_right, frame,
                 psi1, far, inten, xb, ks, zs, back):
    tables = (fwd_t, inv_t, left_t)
    entering = [(probe.at[0], psi1_own.at[0]), (probe.at[1], psi1_own.at[1]), (near, psi1.at[0]), (swapped, psi1.at[1])]

    def leaving(k):
        return leave_mode(k, entering[k][1], far.at[k], window, tables, xb, ks)

    interleave([
        together(
            chain(enter_mode(k, *entering[k], window, kernel, tables, xb, ks, zs), leaving(k)) for k in (2, 3)),
        together(leaving(k) for k in (0, 1)),
    ])
    for rows in chunks():
        terms = []
        for k in range(4):
            re, im = halves(far, k, rows)
            terms.append(re * re + im * im)
        inten[rows, :] = (terms[0] + terms[1]) + (terms[2] + terms[3])
    for rows in chunks():
        inten[rows, :] = (inten[rows, :] * (1.0 / MODES) - patterns[0, rows, :]) * (2.0 / MODES)
    row_base, row_rest = aligned(offsets[0, 0])
    shift = lax.rem(HALO + N + offsets[0, 1], FRAME)
    interleave(
        together(
            backward_mode(k, *entering[k], far.at[k], inten, window, kernel, tables, back, xb, ks, zs) for k in pair)
        for pair in ((0, 1), (2, 3)))
    low = lanes((HALO, 2 * HALO)) < HALO
    zero = jnp.zeros((HALO, 2 * HALO), F32)
    gap = jnp.zeros((8, FRAME), F32)
    for q in range(4):
        s, part = divmod(q, 2)
        for rows in chunks(N, 64):
            columns = slice(part * N, (part + 1) * N)
            block = back[0, s, rows, columns] + back[1, s, rows, columns]
            block = pltpu.roll(jnp.concatenate([block, zero], 1), shift, 1)
            block = pltpu.roll(jnp.concatenate([block, gap], 0), row_rest, 0)
            frame[q, pl.ds(row_base + rows.start, 72), :] += block
    for s in range(2):
        for part in range(2):
            q = 2 * s + part
            gradient[s, part] = frame[q, HALO : HALO + N, 0:N] + REG_WEIGHT * obj[s, part]
            row_top[s, part] = frame[q, 0:HALO, 0:N]
            row_bottom[s, part] = frame[q, HALO + N : FRAME, 0:N]

        def strips(rows):
            re, im = frame[2 * s, rows, N:FRAME], frame[2 * s + 1, rows, N:FRAME]
            right = jnp.where(low, re, pltpu.roll(im, HALO, 1))
            left = jnp.where(low, pltpu.roll(re, HALO, 1), im)
            return right, left

        for rows in chunks(N, HALO):
            right, left = strips(slice(HALO + rows.start, HALO + rows.stop))
            col_right[s, rows] = right
            col_left[s, rows] = left
        corner_right[s, 0], corner_left[s, 0] = strips(slice(HALO + N, FRAME))
        corner_right[s, 1], corner_left[s, 1] = strips(slice(0, HALO))


def put_rows(out, first_row, sums):
    for k, value in enumerate(sums):
        out[first_row + k : first_row + k + 1, :] = jnp.sum(value, axis=0, keepdims=True)


def fold(value):
    rows = value.shape[0]
    value = value[:, : N // 2] + value[:, N // 2 :]
    return sum(value[r : r + 8] for r in range(0, rows, 8))


def accumulate(terms, count, out):
    def body(k, carry):
        rows = pl.ds((k % (N // 16)) * 16, 16)
        q = k // (N // 16)
        return tuple(a + fold(b) for a, b in zip(carry, terms(q // 2, q % 2, rows)))

    zero = tuple(jnp.zeros((8, N // 2), F32) for _ in range(count))
    put_rows(out, 0, lax.fori_loop(0, 4 * (N // 16), body, zero, unroll=2))


def gram_kernel(steps, changes, after, out):
    def terms(s, part, rows):
        st = [steps[i, s, part, rows, :].astype(F32) for i in range(MEM)]
        ch = [changes[i, s, part, rows, :].astype(F32) for i in range(MEM)]
        return [st[i] * ch[j] for i, j in SY_PAIRS] + [ch[i] * ch[j] for i, j in SY_PAIRS]

    accumulate(terms, 2 * len(SY_PAIRS), out)


def dots_kernel(gradient_in, row_up, row_down, col_left, col_right, steps, changes,
                gram, gradient, out, stored, sums, sem):
    low = lanes((64, 2 * HALO)) < HALO
    for s in range(2):
        for part in range(2):
            for rows in chunks(N, 64):
                now = gradient_in[s, part, rows, :]
                if rows.start == 0:
                    now = now + row_up[s, part]
                if rows.stop == N:
                    now = now + row_down[s, part]
                a, b = col_left[s, rows], col_right[s, rows]
                if part == 0:
                    b = pltpu.roll(b, HALO, 1)
                else:
                    a = pltpu.roll(a, HALO, 1)
                gradient[s, part, rows, 0 : 2 * HALO] = now[:, : 2 * HALO] + jnp.where(low, a, 0.0)
                gradient[s, part, rows, N - 2 * HALO : N] = now[:, N - 2 * HALO :] + jnp.where(low, 0.0, b)
    copy = pltpu.make_async_copy(gradient, stored, sem)
    copy.start()

    def body(k, carry):
        q = k // (N // 64)
        rows = pl.ds((k % (N // 64)) * 64, 64)
        s, part = q // 2, q % 2
        g = gradient[s, part, rows, :]
        new = [fold(steps[i, s, part, rows, :].astype(F32) * g) for i in range(MEM)]
        new += [fold(changes[i, s, part, rows, :].astype(F32) * g) for i in range(MEM)]
        return tuple(a + b for a, b in zip(carry, new))

    zero = tuple(jnp.zeros((8, N // 2), F32) for _ in range(2 * MEM))
    sums[0:SG_ROW, :] = gram[0:SG_ROW, :]
    put_rows(sums, SG_ROW, lax.fori_loop(0, 4 * (N // 64), body, zero, unroll=2))
    totals = jnp.sum(sums[...], axis=1, keepdims=True)
    row = lax.broadcasted_iota(jnp.int32, (ROWS, 128), 0)
    spread = jnp.where(row == lanes((ROWS, 128)), totals, 0.0)
    total_row = jnp.sum(spread, axis=0, keepdims=True)
    out[...] = jnp.broadcast_to(total_row[None], (128, 1, 128))
    copy.wait()


def final_kernel(parts, obj, gradient, steps, changes, out, result, sems):
    total = jnp.sum(parts[:, 0, :], axis=0, keepdims=True)
    row = lax.broadcasted_iota(jnp.int32, (ROWS, 128), 0)
    diagonal = jnp.where(row == lanes((ROWS, 128)), total, 0.0)
    splats = jnp.broadcast_to(jnp.sum(diagonal, axis=1, keepdims=True), (ROWS, 128))

    def value(k):
        return splats[k : k + 1, :]

    sy = {pair: value(k) for pair, k in SY_ROW.items()}
    yy = {pair: value(k) for pair, k in YY_ROW.items()}
    inverse = [1.0 / sy[i, i] for i in range(MEM)]
    scaling = sy[MEM - 1, MEM - 1] / yy[MEM - 1, MEM - 1]
    alpha = [None] * MEM
    for i in reversed(range(MEM)):
        term = value(SG_ROW + i)
        for j in reversed(range(i + 1, MEM)):
            term = term - alpha[j] * sy[i, j]
        alpha[i] = term * inverse[i]
    weights = []
    for i in range(MEM):
        term = value(YG_ROW + i)
        for j in reversed(range(MEM)):
            term = term - alpha[j] * yy[min(i, j), max(i, j)]
        term = scaling * term
        for j in range(i):
            term = term + weights[j] * sy[j, i]
        weights.append(alpha[i] - term * inverse[i])

    scale = scaling[0, 0]
    step_weights = [w[0, 0] for w in weights]
    change_weights = [(scaling * a)[0, 0] for a in alpha]
    copies = []
    for s in range(2):
        for part in range(2):

            def body(k, carry):
                rows = pl.ds(k * CHUNK, CHUNK)
                acc = scale * gradient[s, part, rows, :]
                for j in range(MEM):
                    acc = acc - change_weights[j] * changes[j, s, part, rows, :].astype(F32)
                    acc = acc + step_weights[j] * steps[j, s, part, rows, :].astype(F32)
                result[s, part, rows, :] = obj[s, part, rows, :] - acc
                return carry

            lax.fori_loop(0, N // CHUNK, body, 0, unroll=4)
            copies.append(pltpu.make_async_copy(result.at[s, part], out.at[s, part], sems.at[2 * s + part]))
            copies[-1].start()
    for copy in copies:
        copy.wait()


def shape(*dims, dtype=F32):
    return jax.ShapeDtypeStruct(dims, dtype)


def scratch(*dims, dtype=F32):
    return pltpu.VMEM(dims, dtype)


def call(kernel, outs, scratches, args, smem=0, raw=0, stored=(), alias=None):
    return pl.pallas_call(
        kernel,
        out_shape=outs,
        in_specs=[SMEM] * smem + [ANY] * raw + [VMEM] * (len(args) - smem - raw),
        out_specs=tuple(ANY if k in stored else VMEM for k in range(len(outs))),
        scratch_shapes=scratches,
        compiler_params=PARAMS,
        input_output_aliases=alias or {},
    )(*args)


def shifted(value, axis, step):
    size = lax.axis_size(axis)
    return lax.ppermute(value, axis, [(i, (i + step) % size) for i in range(size)])


def near_pairs(rows, modes):
    half = rows // modes
    pairs = []
    for t in range(rows):
        for m in range(modes):
            y = m * modes + t // half
            other = 2 * modes - 1 - y
            target = (other % modes) * half + t % half
            pairs.append((t * modes + m, target * modes + other // modes))
    return pairs


def per_device(object_field, probe, patterns, offsets, phase, past_steps, past_changes):
    rows_axis, modes_axis = lax.axis_size("ty"), lax.axis_size("mode")
    core = (lax.axis_index("ty") & 1).astype(jnp.int32).reshape(1)
    tables = dft_tables()
    first, last = slice(0, HALO), slice(N - HALO, N)
    strip, side, corner = shape(2, 2, HALO, N), shape(2, N, 2 * HALO), shape(2, 2, HALO, 2 * HALO)
    row_first, row_last, col_first, col_last, chosen = call(
        pack_kernel, (strip, strip, side, side, shape(N, 2 * N)),
        [scratch(2, 2, N, 2 * HALO), scratch(2, 2, N, 2 * HALO), pltpu.SemaphoreType.DMA((5,))],
        (core, pltpu.with_memory_space_constraint(object_field, pltpu.HBM),
         pltpu.with_memory_space_constraint(probe, pltpu.HBM)), smem=1, raw=2)
    top = shifted(row_last, "ty", 1)
    bottom = shifted(row_first, "ty", -1)
    left = shifted(col_last, "tx", 1)
    right = shifted(col_first, "tx", -1)
    near = lax.ppermute(chosen, ("ty", "mode"), near_pairs(rows_axis, modes_axis))
    sides = jnp.stack([left, right], 1)
    going_down, going_up = sides[:, :, last], sides[:, :, first]
    corner_up = shifted(going_down, "ty", 1)
    corner_down = shifted(going_up, "ty", -1)
    kernel = jnp.stack([jnp.cos(phase), jnp.sin(phase)])
    whole = shape(4, FRAME + 8, FRAME)
    ext, clear = call(frame_kernel, (whole, whole), [], (object_field, top, bottom, left, right))
    near, ext, clear, corner_up, corner_down, kernel = lax.optimization_barrier(
        (near, ext, clear, corner_up, corner_down, kernel))
    swapped = lax.ppermute(near, "ty", [(i, i ^ 1) for i in range(rows_axis)])

    def work(slots):
        return [scratch(slots, N, 2 * N, dtype=BF16), scratch(slots, 2 * N, 2 * N, dtype=BF16),
                scratch(slots, N, 2 * N)]

    window, psi1, _ = call(
        own_kernel,
        (shape(2, N, 2 * N), shape(2, N, 2 * N), whole),
        work(2),
        (offsets, ext, corner_up, corner_down, probe, kernel) + tables,
        smem=1, alias={1: 2},
    )
    partial, row_top, row_bottom, col_left, col_right, corner_left, corner_right, _ = call(
        other_kernel,
        (shape(2, 2, N, N), strip, strip, side, side, corner, corner, whole),
        [scratch(2, N, 2 * N), scratch(4, N, 2 * N), scratch(N, N)] + work(4)
        + [scratch(2, 2, N, 2 * N)],
        (offsets, object_field, probe, near, swapped, kernel) + tables
        + (patterns, window, psi1, clear),
        smem=1, alias={12: 7},
    )
    from_left = shifted(corner_right, "tx", 1)
    from_right = shifted(corner_left, "tx", -1)
    side_left = shifted(col_right, "tx", 1)
    side_right = shifted(col_left, "tx", -1)

    def with_corners(strip_now, k):
        def unpacked(block):
            return jnp.stack([block[:, k, :, :HALO], block[:, k, :, HALO:]], 1)

        gap = jnp.zeros(strip_now.shape[:3] + (N - 2 * HALO,), F32)
        return strip_now + jnp.concatenate([unpacked(from_left), gap, unpacked(from_right)], -1)

    below, above = with_corners(row_bottom, 0), with_corners(row_top, 1)
    row_up = shifted(below, "ty", 1)
    row_down = shifted(above, "ty", -1)
    gram = call(gram_kernel, (shape(32, 128),), [], (past_steps, past_changes, above))[0]
    gradient, sums, stored = call(
        dots_kernel,
        (shape(2, 2, N, N), shape(128, 1, 128), shape(2, 2, N, N)),
        [scratch(ROWS, 128), pltpu.SemaphoreType.DMA],
        (partial, row_up, row_down, side_left, side_right, past_steps, past_changes,
         gram),
        stored=(2,),
    )
    parts = lax.all_to_all(sums, TILES, 0, 0)
    new_object = call(
        final_kernel, (shape(2, 2, N, N),), [scratch(2, 2, N, N), pltpu.SemaphoreType.DMA((4,))],
        (parts, object_field, gradient, past_steps, past_changes), stored=(0,))[0]
    return (new_object, stored)


def solution(mesh):
    placed = (
        P(None, None, "ty", "tx"),
        P("mode", None, None),
        P(TILES, None, None),
        P(TILES, None),
        P(),
        P(None, None, None, "ty", "tx"),
        P(None, None, None, "ty", "tx"),
    )
    return jax.shard_map(
        per_device,
        mesh=mesh,
        in_specs=placed,
        out_specs=(P(None, None, "ty", "tx"), P(None, None, "ty", "tx")),
        check_vma=False,
    )
```

```python
import math

import jax
import jax.numpy as jnp
import numpy as np
from jax import lax
from jax.experimental import pallas as pl
from jax.experimental.pallas import tpu as pltpu
from jax.sharding import PartitionSpec as P

MODES = 4
HALO = 64
REG_WEIGHT = 1.0
N = 256
FRAME = N + 2 * HALO
MEM = 5
CHUNK = 32
F32 = jnp.float32
BF16 = jnp.bfloat16
TILES = ("ty", "tx")
VMEM = pl.BlockSpec(memory_space=pltpu.VMEM)
ANY = pl.BlockSpec(memory_space=pltpu.HBM)
SMEM = pl.BlockSpec(memory_space=pltpu.SMEM)
PARAMS = pltpu.CompilerParams(vmem_limit_bytes=40 * 1024 * 1024)
SY_PAIRS = [(i, j) for i in range(MEM) for j in range(i, MEM)]
SY_ROW = {pair: k for k, pair in enumerate(SY_PAIRS)}
YY_ROW = {pair: len(SY_PAIRS) + k for k, pair in enumerate(SY_PAIRS)}
SG_ROW = 2 * len(SY_PAIRS)
YG_ROW = SG_ROW + MEM
ROWS = YG_ROW + MEM


def dft_tables():
    indices = np.arange(N, dtype=np.int32)
    products = indices[:, None] * indices[None, :] % N
    angles = products.astype(np.float32) * np.float32(2.0 * math.pi / N)
    cosine = (np.cos(angles) / np.float32(math.sqrt(N))).astype(np.float32)
    sine = (np.sin(angles) / np.float32(math.sqrt(N))).astype(np.float32)
    forward = np.block([[cosine, -sine], [sine, cosine]])
    inverse = np.block([[cosine, sine], [-sine, cosine]])
    left = np.concatenate([cosine, sine], 1)
    return tuple(jnp.asarray(t, BF16) for t in (forward, inverse, left))


def lanes(shape):
    return lax.broadcasted_iota(jnp.int32, shape, len(shape) - 1)


def chunks(total=N, step=CHUNK):
    return [slice(c, c + step) for c in range(0, total, step)]


def aligned(offset):
    base = pl.multiple_of((offset // 8) * 8, 8)
    return base, offset - base


def product(a, b, conjugate):
    ar, ai = a
    br, bi = b
    if conjugate:
        return ar * br + ai * bi, ar * bi - ai * br
    return ar * br - ai * bi, ar * bi + ai * br


def halves(ref, index, rows):
    return ref[index, rows, 0:N], ref[index, rows, N : 2 * N]


def first_pass(xb, ks, m, right, inverse):
    y = jnp.dot(xb[m], right[...], preferred_element_type=F32).astype(BF16)
    yr, yi = y[:, :N], y[:, N:]
    ks[m, 0:N, :] = y
    if inverse:
        ks[m, N : 2 * N, 0:N] = -yi
        ks[m, N : 2 * N, N : 2 * N] = yr
    else:
        ks[m, N : 2 * N, 0:N] = yi
        ks[m, N : 2 * N, N : 2 * N] = -yr


def second_pass(ks, m, left):
    return jnp.dot(left[...], ks[m], preferred_element_type=F32)


def propagate(xb, ks, zs, m, kernel, tables, adjoint):
    forward, inverse, left = tables
    first_pass(xb, ks, m, forward, False)
    yield
    zs[m] = second_pass(ks, m, left)
    yield
    for rows in chunks():
        h = (kernel[0, rows, :], kernel[1, rows, :])
        re, im = product(h, halves(zs, m, rows), adjoint)
        xb[m, rows, 0:N] = re.astype(BF16)
        xb[m, rows, N : 2 * N] = im.astype(BF16)
    yield
    first_pass(xb, ks, m, inverse, True)
    yield


def enter_mode(slot, psi0, psi1, window, kernel, tables, xb, ks, zs):
    for rows in chunks():
        re, im = product(halves(window, 0, rows), (psi0[rows, 0:N], psi0[rows, N : 2 * N]), False)
        xb[slot, rows, 0:N] = re.astype(BF16)
        xb[slot, rows, N : 2 * N] = im.astype(BF16)
    yield
    yield from propagate(xb, ks, zs, slot, kernel, tables, False)
    psi1[...] = second_pass(ks, slot, tables[2])
    yield


def leave_mode(slot, psi1, far, window, tables, xb, ks):
    for rows in chunks():
        re, im = product(halves(window, 1, rows), (psi1[rows, 0:N], psi1[rows, N : 2 * N]), False)
        xb[slot, rows, 0:N] = re.astype(BF16)
        xb[slot, rows, N : 2 * N] = im.astype(BF16)
    yield
    first_pass(xb, ks, slot, tables[0], False)
    yield
    far[...] = second_pass(ks, slot, tables[2])
    yield


def chain(*tasks):
    for task in tasks:
        yield from task


def together(tasks):
    tasks = list(tasks)
    while tasks:
        tasks = [task for task in tasks if next(task, tasks) is not tasks]
        if tasks:
            yield


def backward_mode(slot, psi0, psi1, window, kernel, tables, pieces, xb, ks, zs):
    forward, inverse, left = tables
    pair, m = divmod(slot, 2)
    k = slot

    def collect(s, rows, re, im):
        if m:
            re, im = re + pieces[pair, s, rows, 0:N], im + pieces[pair, s, rows, N : 2 * N]
        pieces[pair, s, rows, 0:N] = re
        pieces[pair, s, rows, N : 2 * N] = im

    first_pass(xb, ks, k, inverse, True)
    yield
    zs[k] = second_pass(ks, k, left)
    yield
    for rows in chunks():
        current = halves(zs, k, rows)
        collect(1, rows, *product((psi1[rows, 0:N], psi1[rows, N : 2 * N]), current, True))
        re, im = product(halves(window, 1, rows), current, True)
        xb[k, rows, 0:N] = re.astype(BF16)
        xb[k, rows, N : 2 * N] = im.astype(BF16)
    yield
    yield from propagate(xb, ks, zs, k, kernel, tables, True)
    zs[k] = second_pass(ks, k, left)
    yield
    for rows in chunks():
        collect(0, rows, *product((psi0[rows, 0:N], psi0[rows, N : 2 * N]), halves(zs, k, rows), True))
    yield


def interleave(tasks):
    waiting, running = list(tasks), []
    while waiting or running:
        if waiting:
            running.append(waiting.pop(0))
        running = [task for task in running if next(task, running) is not running]


def pack_kernel(core, obj, probe, row_first, row_last, col_first, col_last, chosen, edge_first, edge_last, sems):
    low = lanes((N, 2 * HALO)) < HALO
    moves = [
        (obj.at[:, :, :, 0 : 2 * HALO], edge_first),
        (obj.at[:, :, :, N - 2 * HALO : N], edge_last),
        (obj.at[:, :, 0:HALO, :], row_first),
        (obj.at[:, :, N - HALO : N, :], row_last),
        (probe.at[core[0]], chosen),
    ]
    copies = [pltpu.make_async_copy(src, dst, sems.at[k]) for k, (src, dst) in enumerate(moves)]
    for copy in copies:
        copy.start()
    copies[0].wait()
    for s in range(2):
        col_first[s] = jnp.where(low, edge_first[s, 0], pltpu.roll(edge_first[s, 1], HALO, 1))
    copies[1].wait()
    for s in range(2):
        col_last[s] = jnp.where(low, pltpu.roll(edge_last[s, 0], HALO, 1), edge_last[s, 1])
    for copy in copies[2:]:
        copy.wait()


def border(right_block, left_block, part):
    low = lanes(right_block.shape) < HALO
    if part == 0:
        return jnp.where(low, right_block, pltpu.roll(left_block, HALO, 1))
    return jnp.where(low, pltpu.roll(right_block, HALO, 1), left_block)


def frame_kernel(obj, top, bottom, left_in, right_in, ext, clear):
    clear[...] = jnp.zeros(clear.shape, F32)
    for s in range(2):
        for part in range(2):
            q = 2 * s + part
            ext[q, 0:HALO, 0:N] = top[s, part]
            ext[q, HALO : HALO + N, 0:N] = obj[s, part]
            ext[q, HALO + N : FRAME, 0:N] = bottom[s, part]
            ext[q, FRAME : FRAME + 8, :] = jnp.zeros((8, FRAME), F32)
            for rows in chunks(N, HALO):
                ext[q, HALO + rows.start : HALO + rows.stop, N:FRAME] = border(
                    right_in[s, rows], left_in[s, rows], part)


def own_kernel(offsets, ext_in, corner_up, corner_down, probe, kernel, fwd_t, inv_t, left_t,
               window, psi1, ext, xb, ks, zs):
    tables = (fwd_t, inv_t, left_t)
    row_base, row_rest = aligned(offsets[0, 0])
    shift = lax.rem(HALO + FRAME - offsets[0, 1], FRAME)
    for s in range(2):
        for part in range(2):
            q = 2 * s + part
            ext[q, 0:HALO, N:FRAME] = border(corner_up[s, 1], corner_up[s, 0], part)
            ext[q, HALO + N : FRAME, N:FRAME] = border(corner_down[s, 1], corner_down[s, 0], part)
            for rows in chunks(N, 64):
                block = ext[q, pl.ds(row_base + rows.start, 72), :]
                block = pltpu.roll(block, lax.rem(72 - row_rest, 72), 0)[:64]
                window[s, rows, part * N : (part + 1) * N] = pltpu.roll(block, shift, 1)[:, :N]
    interleave([together(
        enter_mode(m, probe.at[m], psi1.at[m], window, kernel, tables, xb, ks, zs) for m in range(2))])


def other_kernel(offsets, obj, probe, near, swapped, kernel, fwd_t, inv_t, left_t, patterns, window, psi1_own, clear,
                 gradient, row_top, row_bottom, col_left, col_right, corner_left, corner_right, frame,
                 psi1, far, xb, ks, zs, back):
    tables = (fwd_t, inv_t, left_t)
    entering = [(probe.at[0], psi1_own.at[0]), (probe.at[1], psi1_own.at[1]), (near, psi1.at[0]), (swapped, psi1.at[1])]

    def leaving(k):
        return leave_mode(k, entering[k][1], far.at[k], window, tables, xb, ks)

    interleave([
        together(
            chain(enter_mode(k, *entering[k], window, kernel, tables, xb, ks, zs), leaving(k)) for k in (2, 3)),
        together(leaving(k) for k in (0, 1)),
    ])
    for rows in chunks(N, 16):
        waves = [halves(far, k, rows) for k in range(4)]
        terms = [re * re + im * im for re, im in waves]
        total = (terms[0] + terms[1]) + (terms[2] + terms[3])
        scale = (total * (1.0 / MODES) - patterns[0, rows, :]) * (2.0 / MODES)
        for k, (re, im) in enumerate(waves):
            xb[k, rows, 0:N] = (scale * re).astype(BF16)
            xb[k, rows, N : 2 * N] = (scale * im).astype(BF16)
    row_base, row_rest = aligned(offsets[0, 0])
    shift = lax.rem(HALO + N + offsets[0, 1], FRAME)
    interleave(
        together(
            backward_mode(k, *entering[k], window, kernel, tables, back, xb, ks, zs) for k in pair)
        for pair in ((0, 1), (2, 3)))
    low = lanes((HALO, 2 * HALO)) < HALO
    zero = jnp.zeros((HALO, 2 * HALO), F32)
    gap = jnp.zeros((8, FRAME), F32)
    for q in range(4):
        s, part = divmod(q, 2)
        for rows in chunks(N, 64):
            columns = slice(part * N, (part + 1) * N)
            block = back[0, s, rows, columns] + back[1, s, rows, columns]
            block = pltpu.roll(jnp.concatenate([block, zero], 1), shift, 1)
            block = pltpu.roll(jnp.concatenate([block, gap], 0), row_rest, 0)
            frame[q, pl.ds(row_base + rows.start, 72), :] += block
    for s in range(2):
        for part in range(2):
            q = 2 * s + part
            gradient[s, part] = frame[q, HALO : HALO + N, 0:N] + REG_WEIGHT * obj[s, part]
            row_top[s, part] = frame[q, 0:HALO, 0:N]
            row_bottom[s, part] = frame[q, HALO + N : FRAME, 0:N]

        def strips(rows):
            re, im = frame[2 * s, rows, N:FRAME], frame[2 * s + 1, rows, N:FRAME]
            right = jnp.where(low, re, pltpu.roll(im, HALO, 1))
            left = jnp.where(low, pltpu.roll(re, HALO, 1), im)
            return right, left

        for rows in chunks(N, HALO):
            right, left = strips(slice(HALO + rows.start, HALO + rows.stop))
            col_right[s, rows] = right
            col_left[s, rows] = left
        corner_right[s, 0], corner_left[s, 0] = strips(slice(HALO + N, FRAME))
        corner_right[s, 1], corner_left[s, 1] = strips(slice(0, HALO))


def put_rows(out, first_row, sums):
    for k, value in enumerate(sums):
        out[first_row + k : first_row + k + 1, :] = jnp.sum(value, axis=0, keepdims=True)


def fold(value):
    rows = value.shape[0]
    value = value[:, : N // 2] + value[:, N // 2 :]
    return sum(value[r : r + 8] for r in range(0, rows, 8))


def accumulate(terms, count, out):
    def body(k, carry):
        rows = pl.ds((k % (N // 16)) * 16, 16)
        q = k // (N // 16)
        return tuple(a + fold(b) for a, b in zip(carry, terms(q // 2, q % 2, rows)))

    zero = tuple(jnp.zeros((8, N // 2), F32) for _ in range(count))
    put_rows(out, 0, lax.fori_loop(0, 4 * (N // 16), body, zero, unroll=4))


def gram_kernel(steps, changes, after, out):
    def terms(s, part, rows):
        st = [steps[i, s, part, rows, :].astype(F32) for i in range(MEM)]
        ch = [changes[i, s, part, rows, :].astype(F32) for i in range(MEM)]
        return [st[i] * ch[j] for i, j in SY_PAIRS] + [ch[i] * ch[j] for i, j in SY_PAIRS]

    accumulate(terms, 2 * len(SY_PAIRS), out)


def dots_kernel(gradient_in, row_up, row_down, col_left, col_right, steps, changes,
                gram, gradient, out, stored, sums, sem):
    low = lanes((64, 2 * HALO)) < HALO
    for s in range(2):
        for part in range(2):
            for rows in chunks(N, 64):
                now = gradient_in[s, part, rows, :]
                if rows.start == 0:
                    now = now + row_up[s, part]
                if rows.stop == N:
                    now = now + row_down[s, part]
                a, b = col_left[s, rows], col_right[s, rows]
                if part == 0:
                    b = pltpu.roll(b, HALO, 1)
                else:
                    a = pltpu.roll(a, HALO, 1)
                gradient[s, part, rows, 0 : 2 * HALO] = now[:, : 2 * HALO] + jnp.where(low, a, 0.0)
                gradient[s, part, rows, N - 2 * HALO : N] = now[:, N - 2 * HALO :] + jnp.where(low, 0.0, b)
    copy = pltpu.make_async_copy(gradient, stored, sem)
    copy.start()

    def body(k, carry):
        q = k // (N // 64)
        rows = pl.ds((k % (N // 64)) * 64, 64)
        s, part = q // 2, q % 2
        g = gradient[s, part, rows, :]
        new = [fold(steps[i, s, part, rows, :].astype(F32) * g) for i in range(MEM)]
        new += [fold(changes[i, s, part, rows, :].astype(F32) * g) for i in range(MEM)]
        return tuple(a + b for a, b in zip(carry, new))

    zero = tuple(jnp.zeros((8, N // 2), F32) for _ in range(2 * MEM))
    sums[0:SG_ROW, :] = gram[0:SG_ROW, :]
    put_rows(sums, SG_ROW, lax.fori_loop(0, 4 * (N // 64), body, zero, unroll=4))
    totals = jnp.sum(sums[...], axis=1, keepdims=True)
    row = lax.broadcasted_iota(jnp.int32, (ROWS, 128), 0)
    spread = jnp.where(row == lanes((ROWS, 128)), totals, 0.0)
    total_row = jnp.sum(spread, axis=0, keepdims=True)
    out[...] = jnp.broadcast_to(total_row[None], (128, 1, 128))
    copy.wait()


def final_kernel(parts, obj, gradient, steps, changes, out, result, sems):
    total = jnp.sum(parts[:, 0, :], axis=0, keepdims=True)
    row = lax.broadcasted_iota(jnp.int32, (ROWS, 128), 0)
    diagonal = jnp.where(row == lanes((ROWS, 128)), total, 0.0)
    splats = jnp.broadcast_to(jnp.sum(diagonal, axis=1, keepdims=True), (ROWS, 128))

    def value(k):
        return splats[k : k + 1, :]

    sy = {pair: value(k) for pair, k in SY_ROW.items()}
    yy = {pair: value(k) for pair, k in YY_ROW.items()}
    inverse = [1.0 / sy[i, i] for i in range(MEM)]
    scaling = sy[MEM - 1, MEM - 1] / yy[MEM - 1, MEM - 1]
    alpha = [None] * MEM
    for i in reversed(range(MEM)):
        term = value(SG_ROW + i)
        for j in reversed(range(i + 1, MEM)):
            term = term - alpha[j] * sy[i, j]
        alpha[i] = term * inverse[i]
    weights = []
    for i in range(MEM):
        term = value(YG_ROW + i)
        for j in reversed(range(MEM)):
            term = term - alpha[j] * yy[min(i, j), max(i, j)]
        term = scaling * term
        for j in range(i):
            term = term + weights[j] * sy[j, i]
        weights.append(alpha[i] - term * inverse[i])

    scale = scaling[0, 0]
    step_weights = [w[0, 0] for w in weights]
    change_weights = [(scaling * a)[0, 0] for a in alpha]
    copies = []
    for s in range(2):
        for part in range(2):

            def body(k, carry):
                rows = pl.ds(k * CHUNK, CHUNK)
                acc = scale * gradient[s, part, rows, :]
                for j in range(MEM):
                    acc = acc - change_weights[j] * changes[j, s, part, rows, :].astype(F32)
                    acc = acc + step_weights[j] * steps[j, s, part, rows, :].astype(F32)
                result[s, part, rows, :] = obj[s, part, rows, :] - acc
                return carry

            lax.fori_loop(0, N // CHUNK, body, 0, unroll=8)
            copies.append(pltpu.make_async_copy(result.at[s, part], out.at[s, part], sems.at[2 * s + part]))
            copies[-1].start()
    for copy in copies:
        copy.wait()


def shape(*dims, dtype=F32):
    return jax.ShapeDtypeStruct(dims, dtype)


def scratch(*dims, dtype=F32):
    return pltpu.VMEM(dims, dtype)


def call(kernel, outs, scratches, args, smem=0, raw=0, stored=(), alias=None):
    return pl.pallas_call(
        kernel,
        out_shape=outs,
        in_specs=[SMEM] * smem + [ANY] * raw + [VMEM] * (len(args) - smem - raw),
        out_specs=tuple(ANY if k in stored else VMEM for k in range(len(outs))),
        scratch_shapes=scratches,
        compiler_params=PARAMS,
        input_output_aliases=alias or {},
    )(*args)


def shifted(value, axis, step):
    size = lax.axis_size(axis)
    return lax.ppermute(value, axis, [(i, (i + step) % size) for i in range(size)])


def near_pairs(rows, modes):
    half = rows // modes
    pairs = []
    for t in range(rows):
        for m in range(modes):
            y = m * modes + t // half
            other = 2 * modes - 1 - y
            target = (other % modes) * half + t % half
            pairs.append((t * modes + m, target * modes + other // modes))
    return pairs


def per_device(object_field, probe, patterns, offsets, phase, past_steps, past_changes):
    rows_axis, modes_axis = lax.axis_size("ty"), lax.axis_size("mode")
    core = (lax.axis_index("ty") & 1).astype(jnp.int32).reshape(1)
    tables = dft_tables()
    first, last = slice(0, HALO), slice(N - HALO, N)
    strip, side, corner = shape(2, 2, HALO, N), shape(2, N, 2 * HALO), shape(2, 2, HALO, 2 * HALO)
    row_first, row_last, col_first, col_last, chosen = call(
        pack_kernel, (strip, strip, side, side, shape(N, 2 * N)),
        [scratch(2, 2, N, 2 * HALO), scratch(2, 2, N, 2 * HALO), pltpu.SemaphoreType.DMA((5,))],
        (core, pltpu.with_memory_space_constraint(object_field, pltpu.HBM),
         pltpu.with_memory_space_constraint(probe, pltpu.HBM)), smem=1, raw=2)
    top = shifted(row_last, "ty", 1)
    bottom = shifted(row_first, "ty", -1)
    left = shifted(col_last, "tx", 1)
    right = shifted(col_first, "tx", -1)
    near = lax.ppermute(chosen, ("ty", "mode"), near_pairs(rows_axis, modes_axis))
    sides = jnp.stack([left, right], 1)
    going_down, going_up = sides[:, :, last], sides[:, :, first]
    corner_up = shifted(going_down, "ty", 1)
    corner_down = shifted(going_up, "ty", -1)
    kernel = jnp.stack([jnp.cos(phase), jnp.sin(phase)])
    whole = shape(4, FRAME + 8, FRAME)
    ext, clear = call(frame_kernel, (whole, whole), [], (object_field, top, bottom, left, right))
    near, ext, clear, corner_up, corner_down, kernel = lax.optimization_barrier(
        (near, ext, clear, corner_up, corner_down, kernel))
    swapped = lax.ppermute(near, "ty", [(i, i ^ 1) for i in range(rows_axis)])

    def work(slots):
        return [scratch(slots, N, 2 * N, dtype=BF16), scratch(slots, 2 * N, 2 * N, dtype=BF16),
                scratch(slots, N, 2 * N)]

    window, psi1, _ = call(
        own_kernel,
        (shape(2, N, 2 * N), shape(2, N, 2 * N), whole),
        work(2),
        (offsets, ext, corner_up, corner_down, probe, kernel) + tables,
        smem=1, alias={1: 2},
    )
    partial, row_top, row_bottom, col_left, col_right, corner_left, corner_right, _ = call(
        other_kernel,
        (shape(2, 2, N, N), strip, strip, side, side, corner, corner, whole),
        [scratch(2, N, 2 * N), scratch(4, N, 2 * N)] + work(4)
        + [scratch(2, 2, N, 2 * N)],
        (offsets, object_field, probe, near, swapped, kernel) + tables
        + (patterns, window, psi1, clear),
        smem=1, alias={12: 7},
    )
    from_left = shifted(corner_right, "tx", 1)
    from_right = shifted(corner_left, "tx", -1)
    side_left = shifted(col_right, "tx", 1)
    side_right = shifted(col_left, "tx", -1)

    def with_corners(strip_now, k):
        def unpacked(block):
            return jnp.stack([block[:, k, :, :HALO], block[:, k, :, HALO:]], 1)

        gap = jnp.zeros(strip_now.shape[:3] + (N - 2 * HALO,), F32)
        return strip_now + jnp.concatenate([unpacked(from_left), gap, unpacked(from_right)], -1)

    below, above = with_corners(row_bottom, 0), with_corners(row_top, 1)
    row_up = shifted(below, "ty", 1)
    row_down = shifted(above, "ty", -1)
    gram = call(gram_kernel, (shape(32, 128),), [], (past_steps, past_changes, above))[0]
    gradient, sums, stored = call(
        dots_kernel,
        (shape(2, 2, N, N), shape(128, 1, 128), shape(2, 2, N, N)),
        [scratch(ROWS, 128), pltpu.SemaphoreType.DMA],
        (partial, row_up, row_down, side_left, side_right, past_steps, past_changes,
         gram),
        stored=(2,),
    )
    parts = lax.all_to_all(sums, TILES, 0, 0)
    new_object = call(
        final_kernel, (shape(2, 2, N, N),), [scratch(2, 2, N, N), pltpu.SemaphoreType.DMA((4,))],
        (parts, object_field, gradient, past_steps, past_changes), stored=(0,))[0]
    return (new_object, stored)


def solution(mesh):
    placed = (
        P(None, None, "ty", "tx"),
        P("mode", None, None),
        P(TILES, None, None),
        P(TILES, None),
        P(),
        P(None, None, None, "ty", "tx"),
        P(None, None, None, "ty", "tx"),
    )
    return jax.shard_map(
        per_device,
        mesh=mesh,
        in_specs=placed,
        out_specs=(P(None, None, "ty", "tx"), P(None, None, "ty", "tx")),
        check_vma=False,
    )
```

```python
import math

import jax
import jax.numpy as jnp
import numpy as np
from jax import lax
from jax.experimental import pallas as pl
from jax.experimental.pallas import tpu as pltpu
from jax.sharding import PartitionSpec as P

MODES = 4
HALO = 64
REG_WEIGHT = 1.0
N = 256
FRAME = N + 2 * HALO
MEM = 5
CHUNK = 32
F32 = jnp.float32
BF16 = jnp.bfloat16
TILES = ("ty", "tx")
VMEM = pl.BlockSpec(memory_space=pltpu.VMEM)
ANY = pl.BlockSpec(memory_space=pltpu.HBM)
SMEM = pl.BlockSpec(memory_space=pltpu.SMEM)
PARAMS = pltpu.CompilerParams(vmem_limit_bytes=40 * 1024 * 1024)
SY_PAIRS = [(i, j) for i in range(MEM) for j in range(i, MEM)]
SY_ROW = {pair: k for k, pair in enumerate(SY_PAIRS)}
YY_ROW = {pair: len(SY_PAIRS) + k for k, pair in enumerate(SY_PAIRS)}
SG_ROW = 2 * len(SY_PAIRS)
YG_ROW = SG_ROW + MEM
ROWS = YG_ROW + MEM


def dft_tables():
    indices = np.arange(N, dtype=np.int32)
    products = indices[:, None] * indices[None, :] % N
    angles = products.astype(np.float32) * np.float32(2.0 * math.pi / N)
    cosine = (np.cos(angles) / np.float32(math.sqrt(N))).astype(np.float32)
    sine = (np.sin(angles) / np.float32(math.sqrt(N))).astype(np.float32)
    forward = np.block([[cosine, -sine], [sine, cosine]])
    inverse = np.block([[cosine, sine], [-sine, cosine]])
    left = np.concatenate([cosine, sine], 1)
    return tuple(jnp.asarray(t, BF16) for t in (forward, inverse, left))


def lanes(shape):
    return lax.broadcasted_iota(jnp.int32, shape, len(shape) - 1)


def chunks(total=N, step=CHUNK):
    return [slice(c, c + step) for c in range(0, total, step)]


def aligned(offset):
    base = pl.multiple_of((offset // 8) * 8, 8)
    return base, offset - base


def product(a, b, conjugate):
    ar, ai = a
    br, bi = b
    if conjugate:
        return ar * br + ai * bi, ar * bi - ai * br
    return ar * br - ai * bi, ar * bi + ai * br


def halves(ref, index, rows):
    return ref[index, rows, 0:N], ref[index, rows, N : 2 * N]


def first_pass(xb, ks, m, right, inverse):
    y = jnp.dot(xb[m], right[...], preferred_element_type=F32).astype(BF16)
    yr, yi = y[:, :N], y[:, N:]
    ks[m, 0:N, :] = y
    if inverse:
        ks[m, N : 2 * N, 0:N] = -yi
        ks[m, N : 2 * N, N : 2 * N] = yr
    else:
        ks[m, N : 2 * N, 0:N] = yi
        ks[m, N : 2 * N, N : 2 * N] = -yr


def second_pass(ks, m, left):
    return jnp.dot(left[...], ks[m], preferred_element_type=F32)


def propagate(xb, ks, zs, m, kernel, tables, adjoint):
    forward, inverse, left = tables
    first_pass(xb, ks, m, forward, False)
    yield
    zs[m] = second_pass(ks, m, left)
    yield
    for rows in chunks():
        h = (kernel[0, rows, :], kernel[1, rows, :])
        re, im = product(h, halves(zs, m, rows), adjoint)
        xb[m, rows, 0:N] = re.astype(BF16)
        xb[m, rows, N : 2 * N] = im.astype(BF16)
    yield
    first_pass(xb, ks, m, inverse, True)
    yield


def enter_mode(slot, psi0, psi1, window, kernel, tables, xb, ks, zs):
    for rows in chunks():
        re, im = product(halves(window, 0, rows), (psi0[rows, 0:N], psi0[rows, N : 2 * N]), False)
        xb[slot, rows, 0:N] = re.astype(BF16)
        xb[slot, rows, N : 2 * N] = im.astype(BF16)
    yield
    yield from propagate(xb, ks, zs, slot, kernel, tables, False)
    psi1[...] = second_pass(ks, slot, tables[2])
    yield


def leave_mode(slot, psi1, far, window, tables, xb, ks):
    for rows in chunks():
        re, im = product(halves(window, 1, rows), (psi1[rows, 0:N], psi1[rows, N : 2 * N]), False)
        xb[slot, rows, 0:N] = re.astype(BF16)
        xb[slot, rows, N : 2 * N] = im.astype(BF16)
    yield
    first_pass(xb, ks, slot, tables[0], False)
    yield
    far[...] = second_pass(ks, slot, tables[2])
    yield


def chain(*tasks):
    for task in tasks:
        yield from task


def together(tasks):
    tasks = list(tasks)
    while tasks:
        tasks = [task for task in tasks if next(task, tasks) is not tasks]
        if tasks:
            yield


def backward_mode(slot, psi0, psi1, window, kernel, tables, pieces, xb, ks, zs):
    forward, inverse, left = tables
    pair, m = divmod(slot, 2)
    k = slot

    def collect(s, rows, re, im):
        if m:
            re, im = re + pieces[pair, s, rows, 0:N], im + pieces[pair, s, rows, N : 2 * N]
        pieces[pair, s, rows, 0:N] = re
        pieces[pair, s, rows, N : 2 * N] = im

    first_pass(xb, ks, k, inverse, True)
    yield
    zs[k] = second_pass(ks, k, left)
    yield
    for rows in chunks():
        current = halves(zs, k, rows)
        collect(1, rows, *product((psi1[rows, 0:N], psi1[rows, N : 2 * N]), current, True))
        re, im = product(halves(window, 1, rows), current, True)
        xb[k, rows, 0:N] = re.astype(BF16)
        xb[k, rows, N : 2 * N] = im.astype(BF16)
    yield
    yield from propagate(xb, ks, zs, k, kernel, tables, True)
    zs[k] = second_pass(ks, k, left)
    yield
    for rows in chunks():
        collect(0, rows, *product((psi0[rows, 0:N], psi0[rows, N : 2 * N]), halves(zs, k, rows), True))
    yield


def interleave(tasks):
    waiting, running = list(tasks), []
    while waiting or running:
        if waiting:
            running.append(waiting.pop(0))
        running = [task for task in running if next(task, running) is not running]


def pack_kernel(core, obj, probe, row_first, row_last, col_first, col_last, chosen, edge_first, edge_last, sems):
    low = lanes((N, 2 * HALO)) < HALO
    moves = [
        (obj.at[:, :, :, 0 : 2 * HALO], edge_first),
        (obj.at[:, :, :, N - 2 * HALO : N], edge_last),
        (obj.at[:, :, 0:HALO, :], row_first),
        (obj.at[:, :, N - HALO : N, :], row_last),
        (probe.at[core[0]], chosen),
    ]
    copies = [pltpu.make_async_copy(src, dst, sems.at[k]) for k, (src, dst) in enumerate(moves)]
    for copy in copies:
        copy.start()
    copies[0].wait()
    for s in range(2):
        col_first[s] = jnp.where(low, edge_first[s, 0], pltpu.roll(edge_first[s, 1], HALO, 1))
    copies[1].wait()
    for s in range(2):
        col_last[s] = jnp.where(low, pltpu.roll(edge_last[s, 0], HALO, 1), edge_last[s, 1])
    for copy in copies[2:]:
        copy.wait()


def border(right_block, left_block, part):
    low = lanes(right_block.shape) < HALO
    if part == 0:
        return jnp.where(low, right_block, pltpu.roll(left_block, HALO, 1))
    return jnp.where(low, pltpu.roll(right_block, HALO, 1), left_block)


def frame_kernel(obj, top, bottom, left_in, right_in, ext, clear):
    clear[...] = jnp.zeros(clear.shape, F32)
    for s in range(2):
        for part in range(2):
            q = 2 * s + part
            ext[q, 0:HALO, 0:N] = top[s, part]
            ext[q, HALO : HALO + N, 0:N] = obj[s, part]
            ext[q, HALO + N : FRAME, 0:N] = bottom[s, part]
            ext[q, FRAME : FRAME + 8, :] = jnp.zeros((8, FRAME), F32)
            for rows in chunks(N, HALO):
                ext[q, HALO + rows.start : HALO + rows.stop, N:FRAME] = border(
                    right_in[s, rows], left_in[s, rows], part)


def own_kernel(offsets, ext_in, corner_up, corner_down, probe, kernel, fwd_t, inv_t, left_t,
               window, psi1, ext, xb, ks, zs):
    tables = (fwd_t, inv_t, left_t)
    row_base, row_rest = aligned(offsets[0, 0])
    shift = lax.rem(HALO + FRAME - offsets[0, 1], FRAME)
    for s in range(2):
        for part in range(2):
            q = 2 * s + part
            ext[q, 0:HALO, N:FRAME] = border(corner_up[s, 1], corner_up[s, 0], part)
            ext[q, HALO + N : FRAME, N:FRAME] = border(corner_down[s, 1], corner_down[s, 0], part)
            for rows in chunks(N, 64):
                block = ext[q, pl.ds(row_base + rows.start, 72), :]
                block = pltpu.roll(block, lax.rem(72 - row_rest, 72), 0)[:64]
                window[s, rows, part * N : (part + 1) * N] = pltpu.roll(block, shift, 1)[:, :N]
    interleave([together(
        enter_mode(m, probe.at[m], psi1.at[m], window, kernel, tables, xb, ks, zs) for m in range(2))])


def other_kernel(offsets, obj, probe, near, swapped, kernel, fwd_t, inv_t, left_t, patterns, window, psi1_own, clear,
                 gradient, row_top, row_bottom, col_left, col_right, corner_left, corner_right, frame,
                 psi1, far, xb, ks, zs, back):
    tables = (fwd_t, inv_t, left_t)
    entering = [(probe.at[0], psi1_own.at[0]), (probe.at[1], psi1_own.at[1]), (near, psi1.at[0]), (swapped, psi1.at[1])]

    def leaving(k):
        return leave_mode(k, entering[k][1], far.at[k], window, tables, xb, ks)

    interleave([
        together(
            chain(enter_mode(k, *entering[k], window, kernel, tables, xb, ks, zs), leaving(k)) for k in (2, 3)),
        together(leaving(k) for k in (0, 1)),
    ])
    for rows in chunks(N, 16):
        waves = [halves(far, k, rows) for k in range(4)]
        terms = [re * re + im * im for re, im in waves]
        total = (terms[0] + terms[1]) + (terms[2] + terms[3])
        scale = (total * (1.0 / MODES) - patterns[0, rows, :]) * (2.0 / MODES)
        for k, (re, im) in enumerate(waves):
            xb[k, rows, 0:N] = (scale * re).astype(BF16)
            xb[k, rows, N : 2 * N] = (scale * im).astype(BF16)
    row_base, row_rest = aligned(offsets[0, 0])
    shift = lax.rem(HALO + N + offsets[0, 1], FRAME)
    interleave(
        together(
            backward_mode(k, *entering[k], window, kernel, tables, back, xb, ks, zs) for k in pair)
        for pair in ((0, 1), (2, 3)))
    low = lanes((HALO, 2 * HALO)) < HALO
    zero = jnp.zeros((HALO, 2 * HALO), F32)
    gap = jnp.zeros((8, FRAME), F32)
    for q in range(4):
        s, part = divmod(q, 2)
        for rows in chunks(N, 64):
            columns = slice(part * N, (part + 1) * N)
            block = back[0, s, rows, columns] + back[1, s, rows, columns]
            block = pltpu.roll(jnp.concatenate([block, zero], 1), shift, 1)
            block = pltpu.roll(jnp.concatenate([block, gap], 0), row_rest, 0)
            frame[q, pl.ds(row_base + rows.start, 8), :] += block[:8]
            frame[q, pl.ds(row_base + rows.start + 8, 64), :] = block[8:]
    for s in range(2):
        for part in range(2):
            q = 2 * s + part
            gradient[s, part] = frame[q, HALO : HALO + N, 0:N] + REG_WEIGHT * obj[s, part]
            row_top[s, part] = frame[q, 0:HALO, 0:N]
            row_bottom[s, part] = frame[q, HALO + N : FRAME, 0:N]

        def strips(rows):
            re, im = frame[2 * s, rows, N:FRAME], frame[2 * s + 1, rows, N:FRAME]
            right = jnp.where(low, re, pltpu.roll(im, HALO, 1))
            left = jnp.where(low, pltpu.roll(re, HALO, 1), im)
            return right, left

        for rows in chunks(N, HALO):
            right, left = strips(slice(HALO + rows.start, HALO + rows.stop))
            col_right[s, rows] = right
            col_left[s, rows] = left
        corner_right[s, 0], corner_left[s, 0] = strips(slice(HALO + N, FRAME))
        corner_right[s, 1], corner_left[s, 1] = strips(slice(0, HALO))


def put_rows(out, first_row, sums):
    for k, value in enumerate(sums):
        out[first_row + k : first_row + k + 1, :] = jnp.sum(value, axis=0, keepdims=True)


def fold(value):
    rows = value.shape[0]
    value = value[:, : N // 2] + value[:, N // 2 :]
    return sum(value[r : r + 8] for r in range(0, rows, 8))


def accumulate(terms, count, out):
    def body(k, carry):
        rows = pl.ds((k % (N // 16)) * 16, 16)
        q = k // (N // 16)
        return tuple(a + fold(b) for a, b in zip(carry, terms(q // 2, q % 2, rows)))

    zero = tuple(jnp.zeros((8, N // 2), F32) for _ in range(count))
    put_rows(out, 0, lax.fori_loop(0, 4 * (N // 16), body, zero, unroll=4))


def gram_kernel(steps, changes, after, out):
    def terms(s, part, rows):
        st = [steps[i, s, part, rows, :].astype(F32) for i in range(MEM)]
        ch = [changes[i, s, part, rows, :].astype(F32) for i in range(MEM)]
        return [st[i] * ch[j] for i, j in SY_PAIRS] + [ch[i] * ch[j] for i, j in SY_PAIRS]

    accumulate(terms, 2 * len(SY_PAIRS), out)


def dots_kernel(gradient_in, row_up, row_down, col_left, col_right, steps, changes,
                gram, gradient, out, stored, sums, sem):
    low = lanes((64, 2 * HALO)) < HALO
    for s in range(2):
        for part in range(2):
            for rows in chunks(N, 64):
                now = gradient_in[s, part, rows, :]
                if rows.start == 0:
                    now = now + row_up[s, part]
                if rows.stop == N:
                    now = now + row_down[s, part]
                a, b = col_left[s, rows], col_right[s, rows]
                if part == 0:
                    b = pltpu.roll(b, HALO, 1)
                else:
                    a = pltpu.roll(a, HALO, 1)
                gradient[s, part, rows, 0 : 2 * HALO] = now[:, : 2 * HALO] + jnp.where(low, a, 0.0)
                gradient[s, part, rows, N - 2 * HALO : N] = now[:, N - 2 * HALO :] + jnp.where(low, 0.0, b)
    copy = pltpu.make_async_copy(gradient, stored, sem)
    copy.start()

    def body(k, carry):
        q = k // (N // 64)
        rows = pl.ds((k % (N // 64)) * 64, 64)
        s, part = q // 2, q % 2
        g = gradient[s, part, rows, :]
        new = [fold(steps[i, s, part, rows, :].astype(F32) * g) for i in range(MEM)]
        new += [fold(changes[i, s, part, rows, :].astype(F32) * g) for i in range(MEM)]
        return tuple(a + b for a, b in zip(carry, new))

    zero = tuple(jnp.zeros((8, N // 2), F32) for _ in range(2 * MEM))
    sums[0:SG_ROW, :] = gram[0:SG_ROW, :]
    put_rows(sums, SG_ROW, lax.fori_loop(0, 4 * (N // 64), body, zero, unroll=4))
    totals = jnp.sum(sums[...], axis=1, keepdims=True)
    row = lax.broadcasted_iota(jnp.int32, (ROWS, 128), 0)
    spread = jnp.where(row == lanes((ROWS, 128)), totals, 0.0)
    total_row = jnp.sum(spread, axis=0, keepdims=True)
    out[...] = jnp.broadcast_to(total_row[None], (128, 1, 128))
    copy.wait()


def final_kernel(parts, obj, gradient, steps, changes, out, result, sems):
    total = jnp.sum(parts[:, 0, :], axis=0, keepdims=True)
    row = lax.broadcasted_iota(jnp.int32, (ROWS, 128), 0)
    diagonal = jnp.where(row == lanes((ROWS, 128)), total, 0.0)
    splats = jnp.broadcast_to(jnp.sum(diagonal, axis=1, keepdims=True), (ROWS, 128))

    def value(k):
        return splats[k : k + 1, :]

    sy = {pair: value(k) for pair, k in SY_ROW.items()}
    yy = {pair: value(k) for pair, k in YY_ROW.items()}
    inverse = [1.0 / sy[i, i] for i in range(MEM)]
    scaling = sy[MEM - 1, MEM - 1] / yy[MEM - 1, MEM - 1]
    alpha = [None] * MEM
    for i in reversed(range(MEM)):
        term = value(SG_ROW + i)
        for j in reversed(range(i + 1, MEM)):
            term = term - alpha[j] * sy[i, j]
        alpha[i] = term * inverse[i]
    weights = []
    for i in range(MEM):
        term = value(YG_ROW + i)
        for j in reversed(range(MEM)):
            term = term - alpha[j] * yy[min(i, j), max(i, j)]
        term = scaling * term
        for j in range(i):
            term = term + weights[j] * sy[j, i]
        weights.append(alpha[i] - term * inverse[i])

    scale = scaling[0, 0]
    step_weights = [w[0, 0] for w in weights]
    change_weights = [(scaling * a)[0, 0] for a in alpha]
    copies = []
    for s in range(2):
        for part in range(2):

            def body(k, carry):
                rows = pl.ds(k * CHUNK, CHUNK)
                acc = scale * gradient[s, part, rows, :]
                for j in range(MEM):
                    acc = acc - change_weights[j] * changes[j, s, part, rows, :].astype(F32)
                    acc = acc + step_weights[j] * steps[j, s, part, rows, :].astype(F32)
                result[s, part, rows, :] = obj[s, part, rows, :] - acc
                return carry

            lax.fori_loop(0, N // CHUNK, body, 0, unroll=8)
            copies.append(pltpu.make_async_copy(result.at[s, part], out.at[s, part], sems.at[2 * s + part]))
            copies[-1].start()
    for copy in copies:
        copy.wait()


def shape(*dims, dtype=F32):
    return jax.ShapeDtypeStruct(dims, dtype)


def scratch(*dims, dtype=F32):
    return pltpu.VMEM(dims, dtype)


def call(kernel, outs, scratches, args, smem=0, raw=0, stored=(), alias=None):
    return pl.pallas_call(
        kernel,
        out_shape=outs,
        in_specs=[SMEM] * smem + [ANY] * raw + [VMEM] * (len(args) - smem - raw),
        out_specs=tuple(ANY if k in stored else VMEM for k in range(len(outs))),
        scratch_shapes=scratches,
        compiler_params=PARAMS,
        input_output_aliases=alias or {},
    )(*args)


def shifted(value, axis, step):
    size = lax.axis_size(axis)
    return lax.ppermute(value, axis, [(i, (i + step) % size) for i in range(size)])


def near_pairs(rows, modes):
    half = rows // modes
    pairs = []
    for t in range(rows):
        for m in range(modes):
            y = m * modes + t // half
            other = 2 * modes - 1 - y
            target = (other % modes) * half + t % half
            pairs.append((t * modes + m, target * modes + other // modes))
    return pairs


def per_device(object_field, probe, patterns, offsets, phase, past_steps, past_changes):
    rows_axis, modes_axis = lax.axis_size("ty"), lax.axis_size("mode")
    core = (lax.axis_index("ty") & 1).astype(jnp.int32).reshape(1)
    tables = dft_tables()
    first, last = slice(0, HALO), slice(N - HALO, N)
    strip, side, corner = shape(2, 2, HALO, N), shape(2, N, 2 * HALO), shape(2, 2, HALO, 2 * HALO)
    row_first, row_last, col_first, col_last, chosen = call(
        pack_kernel, (strip, strip, side, side, shape(N, 2 * N)),
        [scratch(2, 2, N, 2 * HALO), scratch(2, 2, N, 2 * HALO), pltpu.SemaphoreType.DMA((5,))],
        (core, pltpu.with_memory_space_constraint(object_field, pltpu.HBM),
         pltpu.with_memory_space_constraint(probe, pltpu.HBM)), smem=1, raw=2)
    top = shifted(row_last, "ty", 1)
    bottom = shifted(row_first, "ty", -1)
    left = shifted(col_last, "tx", 1)
    right = shifted(col_first, "tx", -1)
    near = lax.ppermute(chosen, ("ty", "mode"), near_pairs(rows_axis, modes_axis))
    sides = jnp.stack([left, right], 1)
    going_down, going_up = sides[:, :, last], sides[:, :, first]
    corner_up = shifted(going_down, "ty", 1)
    corner_down = shifted(going_up, "ty", -1)
    kernel = jnp.stack([jnp.cos(phase), jnp.sin(phase)])
    whole = shape(4, FRAME + 8, FRAME)
    ext, clear = call(frame_kernel, (whole, whole), [], (object_field, top, bottom, left, right))
    near, ext, clear, corner_up, corner_down, kernel = lax.optimization_barrier(
        (near, ext, clear, corner_up, corner_down, kernel))
    swapped = lax.ppermute(near, "ty", [(i, i ^ 1) for i in range(rows_axis)])

    def work(slots):
        return [scratch(slots, N, 2 * N, dtype=BF16), scratch(slots, 2 * N, 2 * N, dtype=BF16),
                scratch(slots, N, 2 * N)]

    window, psi1, _ = call(
        own_kernel,
        (shape(2, N, 2 * N), shape(2, N, 2 * N), whole),
        work(2),
        (offsets, ext, corner_up, corner_down, probe, kernel) + tables,
        smem=1, alias={1: 2},
    )
    partial, row_top, row_bottom, col_left, col_right, corner_left, corner_right, _ = call(
        other_kernel,
        (shape(2, 2, N, N), strip, strip, side, side, corner, corner, whole),
        [scratch(2, N, 2 * N), scratch(4, N, 2 * N)] + work(4)
        + [scratch(2, 2, N, 2 * N)],
        (offsets, object_field, probe, near, swapped, kernel) + tables
        + (patterns, window, psi1, clear),
        smem=1, alias={12: 7},
    )
    from_left = shifted(corner_right, "tx", 1)
    from_right = shifted(corner_left, "tx", -1)
    side_left = shifted(col_right, "tx", 1)
    side_right = shifted(col_left, "tx", -1)

    def with_corners(strip_now, k):
        def unpacked(block):
            return jnp.stack([block[:, k, :, :HALO], block[:, k, :, HALO:]], 1)

        gap = jnp.zeros(strip_now.shape[:3] + (N - 2 * HALO,), F32)
        return strip_now + jnp.concatenate([unpacked(from_left), gap, unpacked(from_right)], -1)

    below, above = with_corners(row_bottom, 0), with_corners(row_top, 1)
    row_up = shifted(below, "ty", 1)
    row_down = shifted(above, "ty", -1)
    gram = call(gram_kernel, (shape(32, 128),), [], (past_steps, past_changes, above))[0]
    gradient, sums, stored = call(
        dots_kernel,
        (shape(2, 2, N, N), shape(128, 1, 128), shape(2, 2, N, N)),
        [scratch(ROWS, 128), pltpu.SemaphoreType.DMA],
        (partial, row_up, row_down, side_left, side_right, past_steps, past_changes,
         gram),
        stored=(2,),
    )
    parts = lax.all_to_all(sums, TILES, 0, 0)
    new_object = call(
        final_kernel, (shape(2, 2, N, N),), [scratch(2, 2, N, N), pltpu.SemaphoreType.DMA((4,))],
        (parts, object_field, gradient, past_steps, past_changes), stored=(0,))[0]
    return (new_object, stored)


def solution(mesh):
    placed = (
        P(None, None, "ty", "tx"),
        P("mode", None, None),
        P(TILES, None, None),
        P(TILES, None),
        P(),
        P(None, None, None, "ty", "tx"),
        P(None, None, None, "ty", "tx"),
    )
    return jax.shard_map(
        per_device,
        mesh=mesh,
        in_specs=placed,
        out_specs=(P(None, None, "ty", "tx"), P(None, None, "ty", "tx")),
        check_vma=False,
    )
```
